256 devices in a mesh: vox: 16 (over y, x_lo, core), tm: 16 (over x_hi, z).
Axes of the slice: x: 4 (x_hi: 2, x_lo: 2; x = x_hi * 2 + x_lo), y: 4, z: 8, core: 2. Of those that a mesh axis runs over, the one named last changes fastest.
Arguments:
- spatial: bfloat16 [32, 2, 64, 4096], P(None, None, 'vox', 'tm'), may hold values from -6 to 6
- temporal: bfloat16 [2, 16, 32], P(None, 'tm'), may hold values from -0.75 to 0.75
- coil_sens: bfloat16 [2, 8, 64, 4096], P(None, None, 'vox'), may hold values from -3 to 3
- kspace: bfloat16 [2, 16, 8, 64, 4096], P(None, 'tm', None, None, 'vox'), may hold values from -6 to 6
- sample_mask: int32 [16, 4096], P('tm', 'vox'), may hold values 0 or 1
Outputs:
- gradient: float32 [32, 2, 64, 4096], P(None, None, 'vox', 'tm')
The draws below stay inside these ranges and needn't reach their ends.
Inputs may be any that keep to these rules, and one draw needn't show every extreme that they name: `sample_mask`: 1 marks an acquired phase-encoding line; the readout direction kx is always fully sampled.
All inputs are finite; a program needn't handle non-finite values. No bound on the sum of `sample_mask` on one device may be relied on, other than what follows from the above.
Results may differ from the reference program's by a relative error of at most 0.0003.
Values may be sent and summed in bfloat16 or wider, within the bound.
No kernel may reach another device: no remote copies, remote signals or barrier semaphores. Data moves between devices by JAX's collectives and lax.ppermute only.
A program may use at most 64 MiB of HBM per device.

```python
import jax
import jax.numpy as jnp
from jax import lax

GRID = 64
PLANE = 4096
RANK = 32
COILS = 8
FRAMES = 16


def touch_ends(array, stream_key, smallest, top_value):
    place = [jax.random.randint(jax.random.fold_in(stream_key, axis), (), 0, length) for axis, length in enumerate(array.shape)]
    main_axis = array.shape.index(max(array.shape))
    beside = place[:main_axis] + [(place[main_axis] + 1) % array.shape[main_axis]] + place[main_axis + 1:]
    return array.at[tuple(place)].set(smallest).at[tuple(beside)].set(top_value)


def block_scale(key, dims, cuts, smallest, top_value):
    level, own = 1.0, jax.random.fold_in(key, 6)
    for dim, shards_of in cuts:
        draws = jnp.exp(jax.random.uniform(jax.random.fold_in(own, dim), (shards_of,), jnp.float32, smallest / len(cuts), top_value / len(cuts)))
        level = level * jnp.repeat(draws, dims[dim] // shards_of).reshape([-1 if axis == dim else 1 for axis in range(len(dims))])
    return level


def noise(rng, dims, width, reach, cuts=(), kind=jnp.bfloat16):
    values = jax.random.normal(rng, dims, jnp.float32) * width
    if len(cuts) > 0:
        values = block_scale(rng, dims, cuts, -0.22, 0.18) * values
    return jnp.clip(values, min=-reach, max=reach).astype(kind)


def setup_inputs(seed: int = 0) -> dict:
    splits = jax.random.split(jax.random.key(seed), 6)
    return {
        "spatial": noise(splits[0], (RANK, 2, GRID, PLANE), 1.0, 6.0, ((2, 16), (3, 16))),
        "temporal": noise(splits[1], (2, FRAMES, RANK), 0.125, 0.75, ((1, 16),)),
        "coil_sens": noise(splits[2], (2, COILS, GRID, PLANE), 0.5, 3.0, ((2, 16),)),
        "kspace": noise(splits[3], (2, FRAMES, COILS, GRID, PLANE), 1.0, 6.0, ((1, 16), (4, 16))),
        "sample_mask": touch_ends((jax.random.randint(splits[4], (FRAMES, PLANE), 0, 3) < 1).astype(jnp.int32), jax.random.fold_in(splits[4], 1), 0, 1),
    }


def reference(spatial, temporal, coil_sens, kspace, sample_mask):
    highest = lax.Precision.HIGHEST
    rank_count = spatial.shape[0]
    grid_len = spatial.shape[2]
    l_re = spatial[:, 0].reshape(rank_count, -1)
    l_im = spatial[:, 1].reshape(rank_count, -1)
    t_re = temporal[0]
    t_im = temporal[1]
    x_re = jnp.dot(t_re, l_re, preferred_element_type=jnp.float32) - jnp.dot(t_im, l_im, preferred_element_type=jnp.float32)
    x_im = jnp.dot(t_im, l_re, preferred_element_type=jnp.float32) + jnp.dot(t_re, l_im, preferred_element_type=jnp.float32)
    sens_f = coil_sens.astype(jnp.float32)
    coil_map = lax.complex(sens_f[0], sens_f[1]).reshape(-1, grid_len, grid_len, grid_len)
    frame_data = jnp.moveaxis(kspace, 1, 0)

    def one_frame(frame_items):
        image_re, image_im, measured, frame_mask = frame_items
        image = lax.complex(image_re, image_im).reshape(grid_len, grid_len, grid_len)
        k_values = jnp.fft.fftn(coil_map * image[None], axes=(1, 2, 3), norm="ortho")
        measured = measured.astype(jnp.float32)
        target = lax.complex(measured[0], measured[1]).reshape(-1, grid_len, grid_len, grid_len)
        keep_mask = frame_mask.astype(jnp.float32).reshape(1, 1, grid_len, grid_len)
        adjoint = jnp.fft.ifftn(keep_mask * (k_values - target), axes=(1, 2, 3), norm="ortho")
        combined = jnp.sum(jnp.conj(coil_map) * adjoint, axis=0).reshape(-1)
        return jnp.real(combined), jnp.imag(combined)

    g_re, g_im = lax.map(one_frame, (x_re, x_im, frame_data, sample_mask))
    tf_re = t_re.astype(jnp.float32)
    tf_im = t_im.astype(jnp.float32)
    grad_re = jnp.dot(tf_re.T, g_re, precision=highest, preferred_element_type=jnp.float32) + jnp.dot(tf_im.T, g_im, precision=highest, preferred_element_type=jnp.float32)
    grad_im = jnp.dot(tf_re.T, g_im, precision=highest, preferred_element_type=jnp.float32) - jnp.dot(tf_im.T, g_re, precision=highest, preferred_element_type=jnp.float32)
    return jnp.stack([grad_re, grad_im], axis=1).reshape(rank_count, 2, grid_len, grid_len * grid_len)
```

```python
import math

import jax
import jax.numpy as jnp
import numpy as np
from jax import lax
from jax.experimental import pallas as pl
from jax.experimental.pallas import tpu as pltpu
from jax.sharding import PartitionSpec as P

N = 64
F32 = jnp.float32
BF16 = jnp.bfloat16
UNSEEN = 1e30
SEEN_BELOW = 1e29


def split(table):
    table = np.asarray(table, np.float64)
    high = table.astype(jnp.bfloat16)
    low = (table - high.astype(np.float64)).astype(jnp.bfloat16)
    return np.stack([high, low])


def dft64():
    k = np.arange(N)
    angle = 2.0 * np.pi * (np.outer(k, k) % N) / N
    return np.cos(angle), np.sin(angle)


def x_table():
    cos, sin = dft64()
    table = np.zeros((2, 16, 2, 4, 2, 2, N))
    for c in range(2):
        table[0, :, c, :, c, 0] = cos.reshape(16, 4, N)
        table[0, :, c, :, c, 1] = -sin.reshape(16, 4, N)
        table[1, :, c, :, c, 0] = sin.reshape(16, 4, N)
        table[1, :, c, :, c, 1] = cos.reshape(16, 4, N)
    return split(table.reshape(256, 256) / 8.0)


def z_tables():
    cos, sin = dft64()
    fwd = np.zeros((2, 2, N, 2, 2, N))
    inv = np.zeros((2, 2, N, 2, 2, N))
    for b in range(2):
        fwd[0, b, :, b, 0] = cos
        fwd[1, b, :, b, 0] = sin
        fwd[0, b, :, b, 1] = -sin
        fwd[1, b, :, b, 1] = cos
        inv[b, 0, :, 0, b] = cos
        inv[b, 1, :, 0, b] = -sin
        inv[b, 0, :, 1, b] = sin
        inv[b, 1, :, 1, b] = cos
    return split(fwd.reshape(256, 256) / 64.0), split(inv.reshape(256, 256) / 64.0)


def dot(a, b):
    return jnp.dot(a, b, preferred_element_type=F32)


def halves(value):
    high = value.astype(BF16)
    return high, (value - high.astype(F32)).astype(BF16)


def z_kernel(k_ref, m_ref, t_ref, o_ref):
    data = jnp.concatenate([k_ref[part, 0, c] for c in range(2) for part in range(2)], axis=0)
    out = dot(t_ref[0], data) + dot(t_ref[1], data)
    low_half = lax.broadcasted_iota(jnp.int32, (128, 128), 1) < N
    keep = jnp.broadcast_to(m_ref[...].astype(F32), (8, 256))
    for h in range(2):
        lanes = slice(h * 128, h * 128 + 128)
        re = out[:128, lanes]
        im = out[128:, lanes]
        on = keep[:, lanes]
        on_swap = pltpu.roll(on, N, 1)
        pieces = (
            (jnp.where(low_half, re, pltpu.roll(im, N, 1)), jnp.where(low_half[:8], on, on_swap)),
            (jnp.where(low_half, pltpu.roll(re, N, 1), im), jnp.where(low_half[:8], on_swap, on)),
        )
        for b in range(2):
            value, seen = pieces[b]
            value = value.reshape(16, 8, 128)
            o_ref[:, 0, 2 * h + b] = jnp.where(seen[None] > 0.5, value, UNSEEN)


def z_part(kspace, mask):
    return pl.pallas_call(
        z_kernel,
        grid=(4,),
        in_specs=[
            pl.BlockSpec((2, 1, 2, 64, 256), lambda q: (0, 0, q, 0, 0)),
            pl.BlockSpec((1, 256), lambda q: (0, 0)),
            pl.BlockSpec((2, 256, 256), lambda q: (0, 0, 0)),
        ],
        out_specs=pl.BlockSpec((16, 1, 4, 8, 128), lambda q: (0, q, 0, 0, 0)),
        out_shape=jax.ShapeDtypeStruct((16, 4, 4, 8, 128), F32),
        name="z_part",
    )(kspace, mask, jnp.asarray(x_table()))


def iota(shape, dim):
    return lax.broadcasted_iota(jnp.int32, shape, dim)


def one_hot(test):
    return jnp.where(test, 1.0, 0.0).astype(BF16)


def image_kernel(r_ref, l_ref, o_ref):
    factors = r_ref[:, 0, :].astype(BF16)
    rows = dot(one_hot(iota((128, 16), 0) // 8 == iota((128, 16), 1)), factors).astype(BF16)
    rank = iota((128, 256), 1) // 8
    pick = iota((128, 256), 0)
    re = dot(rows, one_hot(pick == rank))
    im = dot(rows, one_hot(pick == rank + 32))
    part_out = (iota((128, 256), 0) // 4) % 2
    part_in = (iota((128, 256), 1) // 4) % 2
    same_x = iota((128, 256), 0) % 4 == iota((128, 256), 1) % 4
    value = jnp.where(part_out == part_in, re, jnp.where(part_out == 0, -im, im))
    weights = jnp.where(same_x, value, 0.0).astype(BF16)
    o_ref[...] = dot(weights, l_ref[...]).reshape(16, 8, 256)


def image_part(factors, spatial):
    return pl.pallas_call(
        image_kernel,
        out_shape=jax.ShapeDtypeStruct((16, 8, 256), F32),
        name="image_part",
    )(factors, spatial)


def weight_kernel(r_ref, o_ref):
    factors = r_ref[:, 0, :].astype(BF16)
    rank = iota((256, 128), 0) // 8
    pick = iota((256, 128), 1)
    turned = (((1,), (1,)), ((), ()))
    spread = one_hot(iota((16, 128), 1) // 8 == iota((16, 128), 0))

    def expand(test):
        few = lax.dot_general(one_hot(test), factors, turned, preferred_element_type=F32)
        return dot(few.astype(BF16), spread)

    re = expand(pick == rank)
    im = expand(pick == rank + 32)
    part_in = (iota((256, 128), 0) // 4) % 2
    part_out = (iota((256, 128), 1) // 4) % 2
    same_x = iota((256, 128), 0) % 4 == iota((256, 128), 1) % 4
    value = jnp.where(part_out == part_in, re, jnp.where(part_out == 0, -im, im))
    o_ref[...] = jnp.where(same_x, value, 0.0).astype(BF16)


def weight_part(factors):
    return pl.pallas_call(
        weight_kernel,
        out_shape=jax.ShapeDtypeStruct((256, 128), BF16),
        name="weight_part",
    )(factors)


def dft8(x, turn):
    half = math.sqrt(0.5)

    def quarter(value):
        return pltpu.roll(value, N, 1) * turn

    e0, e1, e2, e3 = x[0] + x[4], x[0] - x[4], x[2] + x[6], quarter(x[2] - x[6])
    o0, o1, o2, o3 = x[1] + x[5], x[1] - x[5], x[3] + x[7], quarter(x[3] - x[7])
    f0, f2, f1, f3 = e0 + e2, e0 - e2, e1 + e3, e1 - e3
    p0, p2, p1, p3 = o0 + o2, quarter(o0 - o2), o1 + o3, o1 - o3
    p1 = (p1 + quarter(p1)) * half
    p3 = (quarter(p3) - p3) * half
    return [f0 + p0, f1 + p1, f2 + p2, f3 + p3, f0 - p0, f1 - p1, f2 - p2, f3 - p3]


def twiddle(value, power, turn):
    power %= N
    if power == 0:
        return value
    angle = 2.0 * math.pi * power / N
    return value * math.cos(angle) + pltpu.roll(value, N, 1) * (turn * math.sin(angle))


def main_kernel(s_ref, i_ref, z_ref, f_ref, b_ref, o_ref, t_ref, u_ref, acc_ref):
    q = pl.program_id(0)
    upper = iota((8, 256), 0) < 4
    lane = iota((8, 128), 1)
    fwd = jnp.where(lane < N, 1.0, -1.0)
    inv = -fwd

    def sens(part, yh, h):
        return s_ref[part, 0, :, yh * 256 + h * 128 : yh * 256 + h * 128 + 128].astype(F32)

    for yh in range(16):
        both = i_ref[yh]
        other = pltpu.roll(both, 4, 0)
        x_re = jnp.where(upper, both, other)
        x_im = jnp.where(upper, other, both)
        for h in range(2):
            s_re, s_im = sens(0, yh, h), sens(1, yh, h)
            a, b = x_re[:, h * 128 : h * 128 + 128], x_im[:, h * 128 : h * 128 + 128]
            row = slice(h * 128 + yh * 8, h * 128 + yh * 8 + 8)
            t_ref[row, :128] = s_re * a - s_im * b
            t_ref[row, 128:] = s_re * b + s_im * a

    def along_z(table):
        high, low = halves(t_ref[...])
        t_ref[...] = dot(high, table[0]) + dot(low, table[0]) + dot(high, table[1])

    def tile(y):
        yh, h, b = y // 4, y // 2 % 2, y % 2
        return slice(h * 128 + yh * 8, h * 128 + yh * 8 + 8), slice(b * 128, b * 128 + 128)

    along_z(f_ref)
    for n in range(8):
        out = dft8([t_ref[tile(8 * m + n)] for m in range(8)], fwd)
        for j in range(8):
            u_ref[8 * j + n] = twiddle(out[j], n * j, fwd)
    for j in range(8):
        out = dft8([u_ref[8 * j + n] for n in range(8)], fwd)
        left = []
        for i in range(8):
            k = 8 * i + j
            z = z_ref[k // 4, 0, k % 4]
            left.append(jnp.where(z < SEEN_BELOW, out[i] - z, 0.0))
        out = dft8(left, inv)
        for n in range(8):
            u_ref[8 * j + n] = twiddle(out[n], n * j, inv)
    for n in range(8):
        out = dft8([u_ref[8 * j + n] for j in range(8)], inv)
        for m in range(8):
            t_ref[tile(8 * m + n)] = out[m]
    along_z(b_ref)

    @pl.when(q == 0)
    def _():
        acc_ref[...] = jnp.zeros_like(acc_ref)

    for yh in range(16):
        for h in range(2):
            row = slice(h * 128 + yh * 8, h * 128 + yh * 8 + 8)
            lanes = slice(h * 128, h * 128 + 128)
            s_re, s_im = sens(0, yh, h), sens(1, yh, h)
            a, b = t_ref[row, :128], t_ref[row, 128:]
            acc_ref[yh, 0, :, lanes] += s_re * a + s_im * b
            acc_ref[yh, 1, :, lanes] += s_re * b - s_im * a

    @pl.when(q == 3)
    def _():
        for yh in range(16):
            re, im = acc_ref[yh, 0], acc_ref[yh, 1]
            re = re + pltpu.roll(re, 4, 0)
            im = im + pltpu.roll(im, 4, 0)
            o_ref[yh] = jnp.where(upper, re, im)


def main_part(sens, images, z):
    fwd, inv = z_tables()
    table = pl.BlockSpec((2, 256, 256), lambda q: (0, 0, 0))
    whole = pl.BlockSpec((16, 8, 256), lambda q: (0, 0, 0))
    return pl.pallas_call(
        main_kernel,
        grid=(4,),
        in_specs=[
            pl.BlockSpec((2, 1, 8, 4096), lambda q: (0, q, 0, 0)),
            whole,
            pl.BlockSpec((16, 1, 4, 8, 128), lambda q: (0, q, 0, 0, 0)),
            table,
            table,
        ],
        out_specs=whole,
        out_shape=jax.ShapeDtypeStruct((16, 8, 256), F32),
        scratch_shapes=[
            pltpu.VMEM((256, 256), F32),
            pltpu.VMEM((64, 8, 128), F32),
            pltpu.VMEM((16, 2, 8, 256), F32),
        ],
        name="main_part",
    )(sens, images, z, jnp.asarray(fwd), jnp.asarray(inv))


def last_kernel(w_ref, c_ref, o_ref):
    high, low = halves(c_ref[...].reshape(128, 256))
    w = w_ref[...]
    o_ref[...] = dot(w, high) + dot(w, low)


def last_part(weights, combined):
    return pl.pallas_call(
        last_kernel,
        out_shape=jax.ShapeDtypeStruct((256, 256), F32),
        name="last_part",
    )(weights, combined)


def exchange(value, axis):
    return lax.all_to_all(value, axis, split_axis=0, concat_axis=0, tiled=True)


def per_device(spatial, temporal, coil_sens, kspace, sample_mask):
    own = temporal.astype(F32).reshape(1, 1, 64)
    own = jnp.pad(own, ((0, 0), (0, 0), (0, 64)))
    factors = exchange(jnp.broadcast_to(own, (16, 1, 128)), "tm")
    z = exchange(z_part(kspace, sample_mask), "vox")
    images = exchange(image_part(factors, spatial.reshape(256, 256)), "tm")
    weights = weight_part(factors)
    combined = main_part(coil_sens.reshape(2, 4, 8, 4096), images, z)
    combined = exchange(combined, "tm")
    return last_part(weights, combined).reshape(32, 2, 4, 256)


def solution(mesh):
    placed = (
        P(None, None, "vox", "tm"),
        P(None, "tm", None),
        P(None, None, "vox", None),
        P(None, "tm", None, None, "vox"),
        P("tm", "vox"),
    )
    return jax.shard_map(
        per_device,
        mesh=mesh,
        in_specs=placed,
        out_specs=P(None, None, "vox", "tm"),
        check_vma=False,
    )
```

```python
import math

import jax
import jax.numpy as jnp
import numpy as np
from jax import lax
from jax.experimental import pallas as pl
from jax.experimental.pallas import tpu as pltpu
from jax.sharding import PartitionSpec as P


N = 64
F32 = jnp.float32
BF16 = jnp.bfloat16
VMEM = pl.BlockSpec(memory_space=pltpu.VMEM)
CODE_SHIFT = 60.0
CODE_SCALE = 2.0**60
UNSEEN = 3e38
SEEN_BELOW = 1e37


def split(table):
    table = np.asarray(table, np.float64)
    high = table.astype(jnp.bfloat16)
    low = (table - high.astype(np.float64)).astype(jnp.bfloat16)
    return np.stack([high, low])


def dft64():
    k = np.arange(N)
    angle = 2.0 * np.pi * (np.outer(k, k) % N) / N
    return np.cos(angle), np.sin(angle)


def x_table():
    cos, sin = dft64()
    table = np.zeros((2, 16, 2, 4, 2, 2, N))
    for c in range(2):
        table[0, :, c, :, c, 0] = cos.reshape(16, 4, N)
        table[0, :, c, :, c, 1] = -sin.reshape(16, 4, N)
        table[1, :, c, :, c, 0] = sin.reshape(16, 4, N)
        table[1, :, c, :, c, 1] = cos.reshape(16, 4, N)
    return split(table.reshape(256, 256) / 8.0)


def z_tables():
    cos, sin = dft64()
    fwd = np.zeros((2, 2, N, 2, 2, N))
    inv = np.zeros((2, 2, N, 2, 2, N))
    for b in range(2):
        fwd[0, b, :, b, 0] = cos
        fwd[1, b, :, b, 0] = sin
        fwd[0, b, :, b, 1] = -sin
        fwd[1, b, :, b, 1] = cos
        inv[b, 0, :, 0, b] = cos
        inv[b, 1, :, 0, b] = -sin
        inv[b, 0, :, 1, b] = sin
        inv[b, 1, :, 1, b] = cos
    return split(fwd.reshape(256, 256) / 64.0), split(inv.reshape(256, 256) / 64.0)


def dot(a, b):
    return jnp.dot(a, b, preferred_element_type=F32)


def halves(value):
    high = value.astype(BF16)
    return high, (value - high.astype(F32)).astype(BF16)


def z_kernel(k_ref, m_ref, t_ref, o_ref):
    data = jnp.concatenate([k_ref[part, 0, c] for c in range(2) for part in range(2)], axis=0)
    out = dot(t_ref[0], data) + dot(t_ref[1], data)
    even = out * out
    fourth = even * even
    even = fourth * fourth * even * CODE_SCALE
    out = jnp.where(out < 0.0, -even, even)
    low_half = lax.broadcasted_iota(jnp.int32, (128, 128), 1) < N
    keep = jnp.broadcast_to(m_ref[...].astype(F32), (8, 256))
    for h in range(2):
        lanes = slice(h * 128, h * 128 + 128)
        re = out[:128, lanes]
        im = out[128:, lanes]
        on = keep[:, lanes]
        on_swap = pltpu.roll(on, N, 1)
        pieces = (
            (jnp.where(low_half, re, pltpu.roll(im, N, 1)), jnp.where(low_half[:8], on, on_swap)),
            (jnp.where(low_half, pltpu.roll(re, N, 1), im), jnp.where(low_half[:8], on_swap, on)),
        )
        for b in range(2):
            value, seen = pieces[b]
            value = value.reshape(16, 8, 128)
            o_ref[:, 2 * h + b] = jnp.where(seen[None] > 0.5, value, UNSEEN).astype(BF16)


def z_part(kspace, mask):
    return pl.pallas_call(
        z_kernel,
        grid=(4,),
        in_specs=[
            pl.BlockSpec((2, 1, 2, 64, 256), lambda q: (0, 0, q, 0, 0)),
            pl.BlockSpec((1, 256), lambda q: (0, 0)),
            pl.BlockSpec((2, 256, 256), lambda q: (0, 0, 0)),
        ],
        out_specs=pl.BlockSpec((16, 4, 8, 128), lambda q: (0, q, 0, 0)),
        out_shape=jax.ShapeDtypeStruct((16, 17, 8, 128), BF16),
        name="z_part",
    )(kspace, mask, jnp.asarray(x_table()))


def factor_kernel(r_ref, z_ref, o_ref, row_ref, tile_ref, sem):
    del z_ref
    row_ref[...] = jnp.zeros_like(row_ref)
    row_ref[0:1, :32] = r_ref[0].astype(F32)
    row_ref[1:2, :32] = r_ref[1].astype(F32)
    re = jnp.broadcast_to(row_ref[0:1, :], (8, 128))
    im = jnp.broadcast_to(row_ref[1:2, :], (8, 128))
    upper = iota((8, 128), 0) < 4
    tile = jnp.where(upper, re, im) + pltpu.roll(jnp.where(upper, -im, re), 32, 1)
    tile_ref[...] = jnp.broadcast_to(tile.astype(BF16)[None, None], (16, 1, 8, 128))
    copy = pltpu.make_async_copy(tile_ref, o_ref.at[:, 16:17], sem)
    copy.start()
    copy.wait()


def add_factors(factors, z):
    return pl.pallas_call(
        factor_kernel,
        in_specs=[VMEM, pl.BlockSpec(memory_space=pl.ANY)],
        out_specs=pl.BlockSpec(memory_space=pl.ANY),
        out_shape=jax.ShapeDtypeStruct((16, 17, 8, 128), BF16),
        scratch_shapes=[
            pltpu.VMEM((8, 128), F32),
            pltpu.VMEM((16, 1, 8, 128), BF16),
            pltpu.SemaphoreType.DMA,
        ],
        input_output_aliases={1: 0},
        name="add_factors",
    )(factors, z)


def iota(shape, dim):
    return lax.broadcasted_iota(jnp.int32, shape, dim)


def one_hot(test):
    return jnp.where(test, 1.0, 0.0).astype(BF16)


def factor_rows(r_ref):
    t = lax.axis_index("tm")
    tiles = [r_ref[lax.rem(f - t + 16, 16), 16].astype(F32) for f in range(16)]
    return jnp.concatenate(tiles, axis=0).astype(BF16)


def image_kernel(r_ref, l_ref, o_ref):
    column = iota((128, 256), 1)
    pick = iota((128, 256), 0) == column // 8 + column // 4 % 2 * 32
    weights = dot(factor_rows(r_ref), one_hot(pick))
    same_x = iota((128, 256), 0) % 4 == column % 4
    weights = jnp.where(same_x, weights, 0.0).astype(BF16)
    o_ref[...] = dot(weights, l_ref[...]).reshape(16, 8, 256)


def image_part(received, spatial):
    return pl.pallas_call(
        image_kernel,
        in_specs=[VMEM, VMEM],
        out_specs=VMEM,
        out_shape=jax.ShapeDtypeStruct((16, 8, 256), F32),
        name="image_part",
    )(received, spatial)


def prepare_kernel(r_ref, w_ref, z_ref):
    row = iota((256, 128), 0)
    pick = iota((256, 128), 1) == row // 8 + row // 4 % 2 * 32
    weights = lax.dot_general(
        one_hot(pick), factor_rows(r_ref), (((1,), (1,)), ((), ())), preferred_element_type=F32
    )
    same_x = row % 4 == iota((256, 128), 1) % 4
    w_ref[...] = jnp.where(same_x, weights, 0.0).astype(BF16)

    def decode(v, carry):
        code = r_ref[v, :16].astype(F32)
        size = jnp.abs(code)
        root = jnp.exp2((jnp.log2(size) - CODE_SHIFT) * 0.1)
        root = jnp.where(size > 0.0, root, 0.0)
        root = jnp.where(code < 0.0, -root, root)
        z_ref[v] = jnp.where(size < SEEN_BELOW, root, UNSEEN)
        return carry

    lax.fori_loop(0, 16, decode, 0)


def prepare_part(received):
    return pl.pallas_call(
        prepare_kernel,
        in_specs=[VMEM],
        out_specs=[VMEM, VMEM],
        out_shape=[
            jax.ShapeDtypeStruct((256, 128), BF16),
            jax.ShapeDtypeStruct((16, 16, 8, 128), F32),
        ],
        name="prepare_part",
    )(received)


def dft8(x, turn):
    half = math.sqrt(0.5)

    def quarter(value):
        return pltpu.roll(value, N, 1) * turn

    e0, e1, e2, e3 = x[0] + x[4], x[0] - x[4], x[2] + x[6], quarter(x[2] - x[6])
    o0, o1, o2, o3 = x[1] + x[5], x[1] - x[5], x[3] + x[7], quarter(x[3] - x[7])
    f0, f2, f1, f3 = e0 + e2, e0 - e2, e1 + e3, e1 - e3
    p0, p2, p1, p3 = o0 + o2, quarter(o0 - o2), o1 + o3, o1 - o3
    p1 = (p1 + quarter(p1)) * half
    p3 = (quarter(p3) - p3) * half
    return [f0 + p0, f1 + p1, f2 + p2, f3 + p3, f0 - p0, f1 - p1, f2 - p2, f3 - p3]


def twiddle(value, power, turn):
    power %= N
    if power == 0:
        return value
    angle = 2.0 * math.pi * power / N
    return value * math.cos(angle) + pltpu.roll(value, N, 1) * (turn * math.sin(angle))


def main_kernel(s_ref, i_ref, z_ref, f_ref, b_ref, o_ref, t_ref, u_ref, acc_ref):
    q = pl.program_id(0)
    upper = iota((8, 256), 0) < 4
    lane = iota((8, 128), 1)
    fwd = jnp.where(lane < N, 1.0, -1.0)
    inv = -fwd

    def sens(part, yh, h):
        return s_ref[part, 0, :, yh * 256 + h * 128 : yh * 256 + h * 128 + 128].astype(F32)

    for yh in range(16):
        both = i_ref[yh]
        other = pltpu.roll(both, 4, 0)
        x_re = jnp.where(upper, both, other)
        x_im = jnp.where(upper, other, both)
        for h in range(2):
            s_re, s_im = sens(0, yh, h), sens(1, yh, h)
            a, b = x_re[:, h * 128 : h * 128 + 128], x_im[:, h * 128 : h * 128 + 128]
            row = slice(h * 128 + yh * 8, h * 128 + yh * 8 + 8)
            t_ref[row, :128] = s_re * a - s_im * b
            t_ref[row, 128:] = s_re * b + s_im * a

    def along_z(table):
        high, low = halves(t_ref[...])
        t_ref[...] = dot(high, table[0]) + dot(low, table[0]) + dot(high, table[1])

    def tile(y):
        yh, h, b = y // 4, y // 2 % 2, y % 2
        return slice(h * 128 + yh * 8, h * 128 + yh * 8 + 8), slice(b * 128, b * 128 + 128)

    along_z(f_ref)
    for n in range(8):
        out = dft8([t_ref[tile(8 * m + n)] for m in range(8)], fwd)
        for j in range(8):
            u_ref[8 * j + n] = twiddle(out[j], n * j, fwd)
    for j in range(8):
        out = dft8([u_ref[8 * j + n] for n in range(8)], fwd)
        left = []
        for i in range(8):
            k = 8 * i + j
            z = z_ref[k // 4, q * 4 + k % 4]
            left.append(jnp.where(z < SEEN_BELOW, out[i] - z, 0.0))
        out = dft8(left, inv)
        for n in range(8):
            u_ref[8 * j + n] = twiddle(out[n], n * j, inv)
    for n in range(8):
        out = dft8([u_ref[8 * j + n] for j in range(8)], inv)
        for m in range(8):
            t_ref[tile(8 * m + n)] = out[m]
    along_z(b_ref)

    @pl.when(q == 0)
    def _():
        acc_ref[...] = jnp.zeros_like(acc_ref)

    for yh in range(16):
        for h in range(2):
            row = slice(h * 128 + yh * 8, h * 128 + yh * 8 + 8)
            lanes = slice(h * 128, h * 128 + 128)
            s_re, s_im = sens(0, yh, h), sens(1, yh, h)
            a, b = t_ref[row, :128], t_ref[row, 128:]
            acc_ref[yh, 0, :, lanes] += s_re * a + s_im * b
            acc_ref[yh, 1, :, lanes] += s_re * b - s_im * a

    @pl.when(q == 3)
    def _():
        for yh in range(16):
            re, im = acc_ref[yh, 0], acc_ref[yh, 1]
            re = re + pltpu.roll(re, 4, 0)
            im = im + pltpu.roll(im, 4, 0)
            o_ref[yh] = jnp.where(upper, re, im)


def main_part(sens, images, z):
    fwd, inv = z_tables()
    table = pl.BlockSpec((2, 256, 256), lambda q: (0, 0, 0))
    return pl.pallas_call(
        main_kernel,
        grid=(4,),
        in_specs=[
            pl.BlockSpec((2, 1, 8, 4096), lambda q: (0, q, 0, 0)),
            VMEM,
            VMEM,
            table,
            table,
        ],
        out_specs=VMEM,
        out_shape=jax.ShapeDtypeStruct((16, 8, 256), F32),
        scratch_shapes=[
            pltpu.VMEM((256, 256), F32),
            pltpu.VMEM((64, 8, 128), F32),
            pltpu.VMEM((16, 2, 8, 256), F32),
        ],
        name="main_part",
    )(sens, images, z, jnp.asarray(fwd), jnp.asarray(inv))


def last_kernel(w_ref, c_ref, o_ref):
    high, low = halves(c_ref[...].reshape(128, 256))
    w = w_ref[...]
    out = dot(w, high) + dot(w, low)
    for r in range(32):
        for part in range(2):
            row = r * 8 + part * 4
            o_ref[r, part] = out[row : row + 4]


def last_part(weights, combined):
    return pl.pallas_call(
        last_kernel,
        in_specs=[VMEM, VMEM],
        out_specs=VMEM,
        out_shape=jax.ShapeDtypeStruct((32, 2, 4, 256), F32),
        name="last_part",
    )(weights, combined)


def exchange(value, axis):
    return lax.all_to_all(value, axis, split_axis=0, concat_axis=0, tiled=True)


def per_device(spatial, temporal, coil_sens, kspace, sample_mask):
    skew = [(j * 16 + (t + j) % 16, j * 16 + t) for j in range(16) for t in range(16)]
    factors = lax.ppermute(temporal, ("vox", "tm"), skew)
    z = z_part(kspace, sample_mask)
    z = add_factors(factors, z)
    received = exchange(z, "vox")
    images = image_part(received, spatial.reshape(256, 256))
    images = exchange(images, "tm")
    weights, z = prepare_part(received)
    combined = main_part(coil_sens.reshape(2, 4, 8, 4096), images, z)
    combined = exchange(combined, "tm")
    return last_part(weights, combined)


def solution(mesh):
    placed = (
        P(None, None, "vox", "tm"),
        P(None, "tm", None),
        P(None, None, "vox", None),
        P(None, "tm", None, None, "vox"),
        P("tm", "vox"),
    )
    return jax.shard_map(
        per_device,
        mesh=mesh,
        in_specs=placed,
        out_specs=P(None, None, "vox", "tm"),
        check_vma=False,
    )
```

```python
import math

import jax
import jax.numpy as jnp
import numpy as np
from jax import lax
from jax.experimental import pallas as pl
from jax.experimental.pallas import tpu as pltpu
from jax.sharding import PartitionSpec as P


N = 64
F32 = jnp.float32
BF16 = jnp.bfloat16
VMEM = pl.BlockSpec(memory_space=pltpu.VMEM)
CODE_SHIFT = 60.0
CODE_SCALE = 2.0**60
UNSEEN = 3e38
SEEN_BELOW = 1e37


def split(table):
    table = np.asarray(table, np.float64)
    high = table.astype(jnp.bfloat16)
    low = (table - high.astype(np.float64)).astype(jnp.bfloat16)
    return np.stack([high, low])


def dft64():
    k = np.arange(N)
    angle = 2.0 * np.pi * (np.outer(k, k) % N) / N
    return np.cos(angle), np.sin(angle)


def x_table():
    cos, sin = dft64()
    table = np.zeros((2, 16, 2, 4, 2, 2, N))
    for c in range(2):
        table[0, :, c, :, c, 0] = cos.reshape(16, 4, N)
        table[0, :, c, :, c, 1] = -sin.reshape(16, 4, N)
        table[1, :, c, :, c, 0] = sin.reshape(16, 4, N)
        table[1, :, c, :, c, 1] = cos.reshape(16, 4, N)
    return split(table.reshape(256, 256) / 8.0)


def z_tables():
    cos, sin = dft64()
    fwd = np.zeros((2, 2, N, 2, 2, N))
    inv = np.zeros((2, 2, N, 2, 2, N))
    for b in range(2):
        fwd[0, b, :, b, 0] = cos
        fwd[1, b, :, b, 0] = sin
        fwd[0, b, :, b, 1] = -sin
        fwd[1, b, :, b, 1] = cos
        inv[b, 0, :, 0, b] = cos
        inv[b, 1, :, 0, b] = -sin
        inv[b, 0, :, 1, b] = sin
        inv[b, 1, :, 1, b] = cos
    return split(fwd.reshape(256, 256) / 64.0), split(inv.reshape(256, 256) / 64.0)


def dot(a, b):
    return jnp.dot(a, b, preferred_element_type=F32)


def halves(value):
    high = value.astype(BF16)
    return high, (value - high.astype(F32)).astype(BF16)


def z_kernel(k_ref, m_ref, t_ref, o_ref):
    data = jnp.concatenate([k_ref[part, 0, c] for c in range(2) for part in range(2)], axis=0)
    out = dot(t_ref[0], data) + dot(t_ref[1], data)
    even = out * out
    fourth = even * even
    even = fourth * fourth * even * CODE_SCALE
    out = jnp.where(out < 0.0, -even, even)
    low_half = lax.broadcasted_iota(jnp.int32, (128, 128), 1) < N
    keep = jnp.broadcast_to(m_ref[...].astype(F32), (8, 256))
    for h in range(2):
        lanes = slice(h * 128, h * 128 + 128)
        re = out[:128, lanes]
        im = out[128:, lanes]
        on = keep[:, lanes]
        on_swap = pltpu.roll(on, N, 1)
        pieces = (
            (jnp.where(low_half, re, pltpu.roll(im, N, 1)), jnp.where(low_half[:8], on, on_swap)),
            (jnp.where(low_half, pltpu.roll(re, N, 1), im), jnp.where(low_half[:8], on_swap, on)),
        )
        for b in range(2):
            value, seen = pieces[b]
            value = value.reshape(16, 8, 128)
            o_ref[:, 2 * h + b] = jnp.where(seen[None] > 0.5, value, UNSEEN).astype(BF16)


def z_part(kspace, mask):
    return pl.pallas_call(
        z_kernel,
        grid=(4,),
        in_specs=[
            pl.BlockSpec((2, 1, 2, 64, 256), lambda q: (0, 0, q, 0, 0)),
            pl.BlockSpec((1, 256), lambda q: (0, 0)),
            pl.BlockSpec((2, 256, 256), lambda q: (0, 0, 0)),
        ],
        out_specs=pl.BlockSpec((16, 4, 8, 128), lambda q: (0, q, 0, 0)),
        out_shape=pltpu.VMEM((16, 17, 8, 128), BF16),
        name="z_part",
    )(kspace, mask, jnp.asarray(x_table()))


def factor_kernel(r_ref, z_ref, o_ref, row_ref, tile_ref, sem):
    del z_ref
    row_ref[...] = jnp.zeros_like(row_ref)
    row_ref[0:1, :32] = r_ref[0, 0:1].astype(F32)
    row_ref[1:2, :32] = r_ref[0, 1:2].astype(F32)
    re = jnp.broadcast_to(row_ref[0:1, :], (8, 128))
    im = jnp.broadcast_to(row_ref[1:2, :], (8, 128))
    upper = iota((8, 128), 0) < 4
    tile = jnp.where(upper, re, im) + pltpu.roll(jnp.where(upper, -im, re), 32, 1)
    tile_ref[...] = jnp.broadcast_to(tile.astype(BF16)[None, None], (16, 1, 8, 128))
    copy = pltpu.make_async_copy(tile_ref, o_ref.at[:, 16:17], sem)
    copy.start()
    copy.wait()


def add_factors(factors, z):
    return pl.pallas_call(
        factor_kernel,
        in_specs=[VMEM, pl.BlockSpec(memory_space=pl.ANY)],
        out_specs=pl.BlockSpec(memory_space=pl.ANY),
        out_shape=pltpu.VMEM((16, 17, 8, 128), BF16),
        scratch_shapes=[
            pltpu.VMEM((8, 128), F32),
            pltpu.VMEM((16, 1, 8, 128), BF16),
            pltpu.SemaphoreType.DMA,
        ],
        input_output_aliases={1: 0},
        name="add_factors",
    )(near(factors), near(z))


def iota(shape, dim):
    return lax.broadcasted_iota(jnp.int32, shape, dim)


def one_hot(test):
    return jnp.where(test, 1.0, 0.0).astype(BF16)


def factor_rows(r_ref):
    t = lax.axis_index("tm")
    tiles = [r_ref[lax.rem(f - t + 16, 16), 16].astype(F32) for f in range(16)]
    return jnp.concatenate(tiles, axis=0).astype(BF16)


def image_kernel(r_ref, l_ref, o_ref):
    column = iota((128, 256), 1)
    pick = iota((128, 256), 0) == column // 8 + column // 4 % 2 * 32
    weights = dot(factor_rows(r_ref), one_hot(pick))
    same_x = iota((128, 256), 0) % 4 == column % 4
    weights = jnp.where(same_x, weights, 0.0).astype(BF16)
    o_ref[...] = dot(weights, l_ref[...]).reshape(16, 8, 256)


def image_part(received, spatial):
    return pl.pallas_call(
        image_kernel,
        in_specs=[VMEM, VMEM],
        out_specs=VMEM,
        out_shape=pltpu.VMEM((16, 8, 256), F32),
        name="image_part",
    )(near(received), near(spatial))


def prepare_kernel(r_ref, w_ref, z_ref):
    row = iota((256, 128), 0)
    pick = iota((256, 128), 1) == row // 8 + row // 4 % 2 * 32
    weights = lax.dot_general(
        one_hot(pick), factor_rows(r_ref), (((1,), (1,)), ((), ())), preferred_element_type=F32
    )
    same_x = row % 4 == iota((256, 128), 1) % 4
    w_ref[...] = jnp.where(same_x, weights, 0.0).astype(BF16)

    def decode(v, carry):
        code = r_ref[v, :16].astype(F32)
        size = jnp.abs(code)
        root = jnp.exp2((jnp.log2(size) - CODE_SHIFT) * 0.1)
        root = jnp.where(size > 0.0, root, 0.0)
        root = jnp.where(code < 0.0, -root, root)
        z_ref[v] = jnp.where(size < SEEN_BELOW, root, UNSEEN)
        return carry

    lax.fori_loop(0, 16, decode, 0)


def prepare_part(received):
    return pl.pallas_call(
        prepare_kernel,
        in_specs=[VMEM],
        out_specs=[VMEM, VMEM],
        out_shape=[
            pltpu.VMEM((256, 128), BF16),
            pltpu.VMEM((16, 16, 8, 128), F32),
        ],
        name="prepare_part",
    )(near(received))


def dft8(x, turn):
    half = math.sqrt(0.5)

    def quarter(value):
        return pltpu.roll(value, N, 1) * turn

    e0, e1, e2, e3 = x[0] + x[4], x[0] - x[4], x[2] + x[6], quarter(x[2] - x[6])
    o0, o1, o2, o3 = x[1] + x[5], x[1] - x[5], x[3] + x[7], quarter(x[3] - x[7])
    f0, f2, f1, f3 = e0 + e2, e0 - e2, e1 + e3, e1 - e3
    p0, p2, p1, p3 = o0 + o2, quarter(o0 - o2), o1 + o3, o1 - o3
    p1 = (p1 + quarter(p1)) * half
    p3 = (quarter(p3) - p3) * half
    return [f0 + p0, f1 + p1, f2 + p2, f3 + p3, f0 - p0, f1 - p1, f2 - p2, f3 - p3]


def twiddle(value, power, turn):
    power %= N
    if power == 0:
        return value
    angle = 2.0 * math.pi * power / N
    return value * math.cos(angle) + pltpu.roll(value, N, 1) * (turn * math.sin(angle))


def main_kernel(s_ref, i_ref, z_ref, f_ref, b_ref, o_ref, t_ref, u_ref, acc_ref):
    q = pl.program_id(0)
    upper = iota((8, 256), 0) < 4
    lane = iota((8, 128), 1)
    fwd = jnp.where(lane < N, 1.0, -1.0)
    inv = -fwd

    def sens(part, yh, h):
        return s_ref[part, 0, :, yh * 256 + h * 128 : yh * 256 + h * 128 + 128].astype(F32)

    for yh in range(16):
        both = i_ref[yh]
        other = pltpu.roll(both, 4, 0)
        x_re = jnp.where(upper, both, other)
        x_im = jnp.where(upper, other, both)
        for h in range(2):
            s_re, s_im = sens(0, yh, h), sens(1, yh, h)
            a, b = x_re[:, h * 128 : h * 128 + 128], x_im[:, h * 128 : h * 128 + 128]
            row = slice(h * 128 + yh * 8, h * 128 + yh * 8 + 8)
            t_ref[row, :128] = s_re * a - s_im * b
            t_ref[row, 128:] = s_re * b + s_im * a

    def along_z(table):
        high, low = halves(t_ref[...])
        t_ref[...] = dot(high, table[0]) + dot(low, table[0]) + dot(high, table[1])

    def tile(y):
        yh, h, b = y // 4, y // 2 % 2, y % 2
        return slice(h * 128 + yh * 8, h * 128 + yh * 8 + 8), slice(b * 128, b * 128 + 128)

    along_z(f_ref)
    for n in range(8):
        out = dft8([t_ref[tile(8 * m + n)] for m in range(8)], fwd)
        for j in range(8):
            u_ref[8 * j + n] = twiddle(out[j], n * j, fwd)
    for j in range(8):
        out = dft8([u_ref[8 * j + n] for n in range(8)], fwd)
        left = []
        for i in range(8):
            k = 8 * i + j
            z = z_ref[k // 4, q * 4 + k % 4]
            left.append(jnp.where(z < SEEN_BELOW, out[i] - z, 0.0))
        out = dft8(left, inv)
        for n in range(8):
            u_ref[8 * j + n] = twiddle(out[n], n * j, inv)
    for n in range(8):
        out = dft8([u_ref[8 * j + n] for j in range(8)], inv)
        for m in range(8):
            t_ref[tile(8 * m + n)] = out[m]
    along_z(b_ref)

    @pl.when(q == 0)
    def _():
        acc_ref[...] = jnp.zeros_like(acc_ref)

    for yh in range(16):
        for h in range(2):
            row = slice(h * 128 + yh * 8, h * 128 + yh * 8 + 8)
            lanes = slice(h * 128, h * 128 + 128)
            s_re, s_im = sens(0, yh, h), sens(1, yh, h)
            a, b = t_ref[row, :128], t_ref[row, 128:]
            acc_ref[yh, 0, :, lanes] += s_re * a + s_im * b
            acc_ref[yh, 1, :, lanes] += s_re * b - s_im * a

    @pl.when(q == 3)
    def _():
        for yh in range(16):
            re, im = acc_ref[yh, 0], acc_ref[yh, 1]
            re = re + pltpu.roll(re, 4, 0)
            im = im + pltpu.roll(im, 4, 0)
            o_ref[yh] = jnp.where(upper, re, im)


def main_part(sens, images, z):
    fwd, inv = z_tables()
    table = pl.BlockSpec((2, 256, 256), lambda q: (0, 0, 0))
    return pl.pallas_call(
        main_kernel,
        grid=(4,),
        in_specs=[
            pl.BlockSpec((2, 1, 8, 4096), lambda q: (0, q, 0, 0)),
            VMEM,
            VMEM,
            table,
            table,
        ],
        out_specs=VMEM,
        out_shape=pltpu.VMEM((16, 8, 256), F32),
        scratch_shapes=[
            pltpu.VMEM((256, 256), F32),
            pltpu.VMEM((64, 8, 128), F32),
            pltpu.VMEM((16, 2, 8, 256), F32),
        ],
        name="main_part",
    )(sens, near(images), near(z), jnp.asarray(fwd), jnp.asarray(inv))


def last_kernel(w_ref, c_ref, o_ref):
    high, low = halves(c_ref[...].reshape(128, 256))
    w = w_ref[...]
    out = dot(w, high) + dot(w, low)
    for r in range(32):
        for part in range(2):
            row = r * 8 + part * 4
            o_ref[r, part] = out[row : row + 4]


def last_part(weights, combined):
    return pl.pallas_call(
        last_kernel,
        in_specs=[VMEM, VMEM],
        out_specs=VMEM,
        out_shape=jax.ShapeDtypeStruct((32, 2, 4, 256), F32),
        name="last_part",
    )(near(weights), near(combined))


def near(value):
    return pltpu.with_memory_space_constraint(value, pltpu.VMEM)


def exchange(value, axis):
    return lax.all_to_all(value, axis, split_axis=0, concat_axis=0, tiled=True)


def per_device(spatial, temporal, coil_sens, kspace, sample_mask):
    skew = [(j * 16 + (t + j) % 16, j * 16 + t) for j in range(16) for t in range(16)]
    factors = lax.ppermute(temporal.transpose(1, 0, 2), ("vox", "tm"), skew)
    z = z_part(kspace, sample_mask)
    z = add_factors(factors, z)
    received = exchange(z, "vox")
    images = image_part(received, spatial.reshape(256, 256))
    images = exchange(images, "tm")
    weights, z = prepare_part(received)
    combined = main_part(coil_sens.reshape(2, 4, 8, 4096), images, z)
    combined = exchange(combined, "tm")
    return last_part(weights, combined)


def solution(mesh):
    placed = (
        P(None, None, "vox", "tm"),
        P(None, "tm", None),
        P(None, None, "vox", None),
        P(None, "tm", None, None, "vox"),
        P("tm", "vox"),
    )
    return jax.shard_map(
        per_device,
        mesh=mesh,
        in_specs=placed,
        out_specs=P(None, None, "vox", "tm"),
        check_vma=False,
    )
```

```python
import math

import jax
import jax.numpy as jnp
import numpy as np
from jax import lax
from jax.experimental import pallas as pl
from jax.experimental.pallas import tpu as pltpu
from jax.sharding import PartitionSpec as P


N = 64
F32 = jnp.float32
BF16 = jnp.bfloat16
VMEM = pl.BlockSpec(memory_space=pltpu.VMEM)
HBM = pl.BlockSpec(memory_space=pl.ANY)
SMALL = pltpu.CompilerParams(vmem_limit_bytes=16 * 2**20)
CODE_SHIFT = 60.0
CODE_SCALE = 2.0**60
UNSEEN = 3e38
SEEN_BELOW = 1e37


def split(table):
    table = np.asarray(table, np.float64)
    high = table.astype(jnp.bfloat16)
    low = (table - high.astype(np.float64)).astype(jnp.bfloat16)
    return high, low


def dft64():
    k = np.arange(N)
    angle = 2.0 * np.pi * (np.outer(k, k) % N) / N
    return np.cos(angle), np.sin(angle)


def x_table():
    cos, sin = dft64()
    table = np.zeros((2, 16, 2, 4, 2, 2, N))
    for c in range(2):
        table[0, :, c, :, c, 0] = cos.reshape(16, 4, N)
        table[0, :, c, :, c, 1] = -sin.reshape(16, 4, N)
        table[1, :, c, :, c, 0] = sin.reshape(16, 4, N)
        table[1, :, c, :, c, 1] = cos.reshape(16, 4, N)
    return np.concatenate(split(table.reshape(256, 256) / 8.0), axis=1)


def z_tables():
    cos, sin = dft64()
    tables = []
    for sign in (1.0, -1.0):
        table = np.zeros((2, 2, N, 2, 2, N))
        for b in range(2):
            table[0, b, :, 0, b] = cos
            table[1, b, :, 0, b] = sign * sin
            table[0, b, :, 1, b] = -sign * sin
            table[1, b, :, 1, b] = cos
        high, low = split(table.reshape(256, 256) / 64.0)
        tables.append(np.concatenate([high, low], axis=0))
    return tables


def y_table():
    n, j, b = np.meshgrid(np.arange(4), np.arange(8), np.arange(128) // N, indexing="ij")
    angle = 2.0 * np.pi * ((2 * n + b) * j % N) / N
    return np.stack([np.cos(angle), np.sin(angle)], axis=2).reshape(64, 128).astype(np.float32)


def dot(a, b):
    return jnp.dot(a, b, preferred_element_type=F32)


def halves(value):
    high = value.astype(BF16)
    return high, (value - high.astype(F32)).astype(BF16)


def z_kernel(k_hbm, m_ref, t_hbm, o_ref, k_ref, t_ref, sems):
    copies = [pltpu.make_async_copy(t_hbm, t_ref, sems.at[4])]
    for q in range(4):
        pair = pl.ds(2 * q, 2)
        copies.append(pltpu.make_async_copy(k_hbm.at[:, :, pair], k_ref.at[:, :, pair], sems.at[q]))
    for copy in copies:
        copy.start()
    for copy in copies:
        copy.wait()
    seen = jnp.broadcast_to(m_ref[...].astype(F32), (8, 256)) > 0.5
    for q in range(4):
        data = [k_ref[part, 0, 2 * q + c] for c in range(2) for part in range(2)]
        out = dot(t_ref[...], jnp.concatenate(data + data, axis=0))
        even = out * out
        fourth = even * even
        even = fourth * fourth * even * CODE_SCALE
        out = jnp.where(out < 0.0, -even, even)
        for part in range(2):
            for h in range(2):
                lanes = slice(h * 128, h * 128 + 128)
                value = out[part * 128 : part * 128 + 128, lanes].reshape(16, 8, 128)
                value = jnp.where(seen[None, :, lanes], value, UNSEEN)
                o_ref[:, 4 * q + 2 * part + h] = value.astype(BF16)


def z_part(kspace, mask):
    return pl.pallas_call(
        z_kernel,
        in_specs=[HBM, VMEM, HBM],
        out_specs=VMEM,
        out_shape=pltpu.VMEM((16, 17, 8, 128), BF16),
        scratch_shapes=[
            pltpu.VMEM(kspace.shape, BF16),
            pltpu.VMEM((256, 512), BF16),
            pltpu.SemaphoreType.DMA((5,)),
        ],
        name="z_part",
        compiler_params=SMALL,
    )(far(kspace), near(mask), far(jnp.asarray(x_table())))


def factor_kernel(r_ref, z_ref, o_ref, row_ref, tile_ref, sem):
    del z_ref
    row_ref[...] = jnp.zeros_like(row_ref)
    row_ref[0:1, :32] = r_ref[0, 0:1].astype(F32)
    row_ref[1:2, :32] = r_ref[0, 1:2].astype(F32)
    re = jnp.broadcast_to(row_ref[0:1, :], (8, 128))
    im = jnp.broadcast_to(row_ref[1:2, :], (8, 128))
    upper = iota((8, 128), 0) < 4
    tile = jnp.where(upper, re, im) + pltpu.roll(jnp.where(upper, -im, re), 32, 1)
    tile_ref[...] = jnp.broadcast_to(tile.astype(BF16)[None, None], (16, 1, 8, 128))
    copy = pltpu.make_async_copy(tile_ref, o_ref.at[:, 16:17], sem)
    copy.start()
    copy.wait()


def add_factors(factors, z):
    return pl.pallas_call(
        factor_kernel,
        in_specs=[VMEM, pl.BlockSpec(memory_space=pl.ANY)],
        out_specs=pl.BlockSpec(memory_space=pl.ANY),
        out_shape=pltpu.VMEM((16, 17, 8, 128), BF16),
        scratch_shapes=[
            pltpu.VMEM((8, 128), F32),
            pltpu.VMEM((16, 1, 8, 128), BF16),
            pltpu.SemaphoreType.DMA,
        ],
        input_output_aliases={1: 0},
        name="add_factors",
        compiler_params=SMALL,
    )(near(factors), near(z))


def iota(shape, dim):
    return lax.broadcasted_iota(jnp.int32, shape, dim)


def one_hot(test):
    return jnp.where(test, 1.0, 0.0).astype(BF16)


def factor_rows(r_ref):
    t = lax.axis_index("tm")
    tiles = [r_ref[lax.rem(f - t + 16, 16), 16].astype(F32) for f in range(16)]
    return jnp.concatenate(tiles, axis=0).astype(BF16)


def image_kernel(r_ref, l_ref, o_ref):
    column = iota((128, 256), 1)
    pick = iota((128, 256), 0) == column // 8 + column // 4 % 2 * 32
    weights = dot(factor_rows(r_ref), one_hot(pick))
    same_x = iota((128, 256), 0) % 4 == column % 4
    weights = jnp.where(same_x, weights, 0.0).astype(BF16)
    o_ref[...] = dot(weights, l_ref[...]).reshape(16, 8, 256)


def image_part(received, spatial):
    return pl.pallas_call(
        image_kernel,
        in_specs=[VMEM, VMEM],
        out_specs=VMEM,
        out_shape=pltpu.VMEM((16, 8, 256), F32),
        name="image_part",
        compiler_params=SMALL,
    )(near(received), near(spatial))


def prepare_kernel(r_ref, w_ref, z_ref):
    row = iota((256, 128), 0)
    pick = iota((256, 128), 1) == row // 8 + row // 4 % 2 * 32
    weights = lax.dot_general(
        one_hot(pick), factor_rows(r_ref), (((1,), (1,)), ((), ())), preferred_element_type=F32
    )
    same_x = row % 4 == iota((256, 128), 1) % 4
    w_ref[...] = jnp.where(same_x, weights, 0.0).astype(BF16)

    low_half = iota((8, 128), 1) < N

    def decode(v, tile):
        code = r_ref[v, tile].astype(F32)
        size = jnp.abs(code)
        root = jnp.exp2((jnp.log2(size) - CODE_SHIFT) * 0.1)
        root = jnp.where(size > 0.0, root, 0.0)
        root = jnp.where(code < 0.0, -root, root)
        return jnp.where(size < SEEN_BELOW, root, UNSEEN)

    def pair(v, carry):
        for q in range(4):
            for part in range(2):
                for h in range(2):
                    a, b = decode(v, 4 * q + 2 * part + h), decode(v + 8, 4 * q + 2 * part + h)
                    z_ref[q, part, 4 * v + 2 * h] = jnp.where(low_half, a, pltpu.roll(b, N, 1))
                    z_ref[q, part, 4 * v + 2 * h + 1] = jnp.where(low_half, pltpu.roll(a, N, 1), b)
        return carry

    lax.fori_loop(0, 8, pair, 0)


def prepare_part(received):
    return pl.pallas_call(
        prepare_kernel,
        in_specs=[VMEM],
        out_specs=[VMEM, VMEM],
        out_shape=[
            pltpu.VMEM((256, 128), BF16),
            pltpu.VMEM((4, 2, 32, 8, 128), F32),
        ],
        name="prepare_part",
        compiler_params=SMALL,
    )(near(received))


def plus(a, b):
    return a[0] + b[0], a[1] + b[1]


def minus(a, b):
    return a[0] - b[0], a[1] - b[1]


def plus_i(a, b, sign):
    if sign > 0:
        return a[0] - b[1], a[1] + b[0]
    return a[0] + b[1], a[1] - b[0]


def times(a, c, s, sign):
    if sign > 0:
        return a[0] * c - a[1] * s, a[1] * c + a[0] * s
    return a[0] * c + a[1] * s, a[1] * c - a[0] * s


def dft4(x, sign):
    a, b, c, d = plus(x[0], x[2]), minus(x[0], x[2]), plus(x[1], x[3]), minus(x[1], x[3])
    return [plus(a, c), plus_i(b, d, sign), minus(a, c), plus_i(b, d, -sign)]


def dft8(x, sign):
    half = math.sqrt(0.5)
    e, o = dft4(x[0::2], sign), dft4(x[1::2], sign)
    p = plus_i(o[1], o[1], sign)
    m = plus_i(o[3], o[3], -sign)
    p = p[0] * half, p[1] * half
    m = m[0] * half, m[1] * half
    return [
        plus(e[0], o[0]),
        plus(e[1], p),
        plus_i(e[2], o[2], sign),
        minus(e[3], m),
        minus(e[0], o[0]),
        minus(e[1], p),
        plus_i(e[2], o[2], -sign),
        plus(e[3], m),
    ]


def main_kernel(s_ref, i_ref, z_ref, f_ref, b_ref, y_ref, o_ref, t_ref, u_ref, acc_ref):
    upper = iota((8, 256), 0) < 4
    low_half = iota((8, 128), 1) < N
    flip = jnp.where(low_half, 1.0, -1.0)
    cos1 = jnp.where(low_half, 1.0, math.sqrt(0.5))
    cos3 = jnp.where(low_half, 1.0, -math.sqrt(0.5))
    sin1 = jnp.where(low_half, 0.0, math.sqrt(0.5))

    def sens(q, part, yh, h):
        at = yh * 256 + h * 128
        return s_ref[part, q, :, at : at + 128].astype(F32)

    def along_z(value, table):
        high, low = halves(value)
        table = jnp.concatenate([table[:256], table[:256], table[256:]], axis=0)
        return dot(jnp.concatenate([high, low, high], axis=1), table)

    def coil_images(q):
        parts = ([], [])
        for h in range(2):
            for yh in range(16):
                both = i_ref[yh, :, h * 128 : h * 128 + 128]
                other = pltpu.roll(both, 4, 0)
                a = jnp.where(upper[:, :128], both, other)
                b = jnp.where(upper[:, :128], other, both)
                s_re, s_im = sens(q, 0, yh, h), sens(q, 1, yh, h)
                parts[0].append(s_re * a - s_im * b)
                parts[1].append(s_re * b + s_im * a)
        value = jnp.concatenate([jnp.concatenate(part, axis=0) for part in parts], axis=1)
        t_ref[q] = along_z(value, f_ref)

    def rows(m, n):
        at = n % 2 * 128 + (2 * m + n // 2) * 8
        return slice(at, at + 8)

    def turn(value, i, sign):
        if i == 0:
            return value
        if i == 2:
            re, im = value
            if sign > 0:
                return jnp.where(low_half, re, -im), jnp.where(low_half, im, re)
            return jnp.where(low_half, re, im), jnp.where(low_half, im, -re)
        return times(value, cos1 if i == 1 else cos3, sin1, sign)

    def wave(n, j):
        at = 2 * (8 * n + j)
        return y_ref[at : at + 1, :], y_ref[at + 1 : at + 2, :]

    def across(value):
        return tuple(part * flip + pltpu.roll(part, N, 1) for part in value)

    def residual(q):
        for n in range(4):
            x = [(t_ref[q, rows(m, n), :128], t_ref[q, rows(m, n), 128:]) for m in range(8)]
            x = dft8(x, -1)
            for j in range(8):
                if j > 0:
                    x[j] = times(x[j], *wave(n, j), -1)
                u_ref[q, 4 * j + n, 0], u_ref[q, 4 * j + n, 1] = x[j]
        for j in range(8):
            x = dft4([(u_ref[q, 4 * j + n, 0], u_ref[q, 4 * j + n, 1]) for n in range(4)], -1)
            for i in range(4):
                re, im = across(turn(x[i], i, -1))
                z_re, z_im = z_ref[q, 0, 8 * i + j], z_ref[q, 1, 8 * i + j]
                seen = z_re < SEEN_BELOW
                left = jnp.where(seen, re - z_re, 0.0), jnp.where(seen, im - z_im, 0.0)
                x[i] = turn(across(left), i, 1)
            x = dft4(x, 1)
            for n in range(4):
                if j > 0:
                    x[n] = times(x[n], *wave(n, j), 1)
                u_ref[q, 4 * j + n, 0], u_ref[q, 4 * j + n, 1] = x[n]
        for n in range(4):
            x = [(u_ref[q, 4 * j + n, 0], u_ref[q, 4 * j + n, 1]) for j in range(8)]
            x = dft8(x, 1)
            for m in range(8):
                t_ref[q, rows(m, n), :128], t_ref[q, rows(m, n), 128:] = x[m]

    def combine(q):
        value = along_z(t_ref[q], b_ref)
        for h in range(2):
            for yh in range(16):
                at = h * 128 + yh * 8
                a, b = value[at : at + 8, :128], value[at : at + 8, 128:]
                s_re, s_im = sens(q, 0, yh, h), sens(q, 1, yh, h)
                re = s_re * a + s_im * b
                im = s_re * b - s_im * a
                if q > 0:
                    re = re + acc_ref[yh, h, 0]
                    im = im + acc_ref[yh, h, 1]
                if q < 3:
                    acc_ref[yh, h, 0] = re
                    acc_ref[yh, h, 1] = im
                else:
                    re = re + pltpu.roll(re, 4, 0)
                    im = im + pltpu.roll(im, 4, 0)
                    o_ref[yh, :, h * 128 : h * 128 + 128] = jnp.where(upper[:, :128], re, im)

    coil_images(0)
    for q in range(4):
        if q < 3:
            coil_images(q + 1)
        residual(q)
        if q > 0:
            combine(q - 1)
    combine(3)


def main_part(sens, images, z):
    fwd, inv = z_tables()
    return pl.pallas_call(
        main_kernel,
        in_specs=[VMEM] * 6,
        out_specs=VMEM,
        out_shape=pltpu.VMEM((16, 8, 256), F32),
        scratch_shapes=[
            pltpu.VMEM((4, 256, 256), F32),
            pltpu.VMEM((4, 32, 2, 8, 128), F32),
            pltpu.VMEM((16, 2, 2, 8, 128), F32),
        ],
        name="main_part",
        compiler_params=SMALL,
    )(
        near(sens),
        near(images),
        near(z),
        near(jnp.asarray(fwd)),
        near(jnp.asarray(inv)),
        near(jnp.asarray(y_table())),
    )


def last_kernel(w_ref, c_ref, o_ref):
    high, low = halves(c_ref[...].reshape(128, 256))
    w = w_ref[...]
    out = dot(w, high) + dot(w, low)
    for r in range(32):
        for part in range(2):
            row = r * 8 + part * 4
            o_ref[r, part] = out[row : row + 4]


def last_part(weights, combined):
    return pl.pallas_call(
        last_kernel,
        in_specs=[VMEM, VMEM],
        out_specs=VMEM,
        out_shape=jax.ShapeDtypeStruct((32, 2, 4, 256), F32),
        name="last_part",
        compiler_params=SMALL,
    )(near(weights), near(combined))


def near(value):
    return pltpu.with_memory_space_constraint(value, pltpu.VMEM)


def far(value):
    return pltpu.with_memory_space_constraint(value, pltpu.HBM)


def exchange(value, axis):
    return lax.all_to_all(value, axis, split_axis=0, concat_axis=0, tiled=True)


def per_device(spatial, temporal, coil_sens, kspace, sample_mask):
    skew = [(j * 16 + (t + j) % 16, j * 16 + t) for j in range(16) for t in range(16)]
    factors = lax.ppermute(temporal.transpose(1, 0, 2), ("vox", "tm"), skew)
    z = z_part(kspace, sample_mask)
    z = add_factors(factors, z)
    received = exchange(z, "vox")
    images = image_part(received, spatial.reshape(256, 256))
    images = exchange(images, "tm")
    weights, z = prepare_part(received)
    combined = main_part(coil_sens.reshape(2, 4, 8, 4096), images, z)
    combined = exchange(combined, "tm")
    return last_part(weights, combined)


def solution(mesh):
    placed = (
        P(None, None, "vox", "tm"),
        P(None, "tm", None),
        P(None, None, "vox", None),
        P(None, "tm", None, None, "vox"),
        P("tm", "vox"),
    )
    return jax.shard_map(
        per_device,
        mesh=mesh,
        in_specs=placed,
        out_specs=P(None, None, "vox", "tm"),
        check_vma=False,
    )
```

```python
import math

import jax
import jax.numpy as jnp
import numpy as np
from jax import lax
from jax.experimental import pallas as pl
from jax.experimental.pallas import tpu as pltpu
from jax.sharding import PartitionSpec as P


N = 64
F32 = jnp.float32
BF16 = jnp.bfloat16
VMEM = pl.BlockSpec(memory_space=pltpu.VMEM)
HBM = pl.BlockSpec(memory_space=pl.ANY)
SMALL = pltpu.CompilerParams(vmem_limit_bytes=16 * 2**20)
Z_SCALE = 2.0**6
UNSEEN = 3e38
SEEN_BELOW = 1e37


def split(table):
    table = np.asarray(table, np.float64)
    high = table.astype(jnp.bfloat16)
    low = (table - high.astype(np.float64)).astype(jnp.bfloat16)
    return high, low


def dft64():
    k = np.arange(N)
    angle = 2.0 * np.pi * (np.outer(k, k) % N) / N
    return np.cos(angle), np.sin(angle)


def x_table():
    cos, sin = dft64()
    table = np.zeros((2, 16, 2, 4, 2, 2, N))
    for c in range(2):
        table[0, :, c, :, c, 0] = cos.reshape(16, 4, N)
        table[0, :, c, :, c, 1] = -sin.reshape(16, 4, N)
        table[1, :, c, :, c, 0] = sin.reshape(16, 4, N)
        table[1, :, c, :, c, 1] = cos.reshape(16, 4, N)
    return np.concatenate(split(table.reshape(256, 256) / 8.0 * Z_SCALE), axis=1)


def z_tables():
    cos, sin = dft64()
    tables = []
    for sign in (1.0, -1.0):
        table = np.zeros((2, 2, N, 2, 2, N))
        for b in range(2):
            table[0, b, :, 0, b] = cos
            table[1, b, :, 0, b] = sign * sin
            table[0, b, :, 1, b] = -sign * sin
            table[1, b, :, 1, b] = cos
        high, low = split(table.reshape(256, 256) / 64.0)
        tables.append(np.concatenate([high, low], axis=0))
    return tables


def y_table():
    n, j, b = np.meshgrid(np.arange(4), np.arange(8), np.arange(128) // N, indexing="ij")
    angle = 2.0 * np.pi * ((2 * n + b) * j % N) / N
    return np.stack([np.cos(angle), np.sin(angle)], axis=2).reshape(64, 128).astype(np.float32)


def dot(a, b):
    return jnp.dot(a, b, preferred_element_type=F32)


def halves(value):
    high = value.astype(BF16)
    return high, (value - high.astype(F32)).astype(BF16)


def load_kernel(l_hbm, k_hbm, m_hbm, t_hbm, l_ref, k_ref, m_ref, t_ref, s_ref, sems):
    copies = [
        pltpu.make_async_copy(l_hbm, s_ref, sems.at[0]),
        pltpu.make_async_copy(m_hbm, m_ref, sems.at[1]),
        pltpu.make_async_copy(t_hbm, t_ref, sems.at[2]),
        pltpu.make_async_copy(k_hbm, k_ref, sems.at[3]),
    ]
    for copy in copies:
        copy.start()
    copies[0].wait()
    for r in range(0, 32, 2):
        rows = [s_ref[r + i // 2, i % 2].astype(F32) for i in range(4)]
        l_ref[8 * r : 8 * r + 16] = jnp.concatenate(rows, axis=0).astype(BF16)
    for copy in copies[1:]:
        copy.wait()


def load_part(spatial, kspace, mask):
    return pl.pallas_call(
        load_kernel,
        in_specs=[HBM] * 4,
        out_specs=[VMEM] * 4,
        out_shape=[
            pltpu.VMEM((256, 256), BF16),
            pltpu.VMEM(kspace.shape, BF16),
            pltpu.VMEM((1, 256), jnp.int32),
            pltpu.VMEM((256, 512), BF16),
        ],
        scratch_shapes=[
            pltpu.VMEM(spatial.shape, BF16),
            pltpu.SemaphoreType.DMA((4,)),
        ],
        name="load_part",
        compiler_params=SMALL,
    )(far(spatial), far(kspace), far(mask), far(jnp.asarray(x_table())))


def encode(value):
    even = value * value
    fourth = even * even
    even = fourth * fourth * even
    return jnp.where(value < 0.0, -even, even)


def decode(code, scale):
    size = jnp.abs(code)
    root = jnp.exp2(jnp.log2(size) * 0.1 - math.log2(scale))
    root = jnp.where(size > 0.0, root, 0.0)
    return jnp.where(code < 0.0, -root, root)


def z_kernel(k_ref, m_ref, t_ref, o_ref):
    seen = jnp.broadcast_to(m_ref[...].astype(F32), (8, 256)) > 0.5
    for q in range(4):
        data = [k_ref[part, 0, 2 * q + c] for c in range(2) for part in range(2)]
        out = dot(t_ref[...], jnp.concatenate(data + data, axis=0))
        out = encode(out)
        for part in range(2):
            for h in range(2):
                lanes = slice(h * 128, h * 128 + 128)
                value = out[part * 128 : part * 128 + 128, lanes].reshape(16, 8, 128)
                value = jnp.where(seen[None, :, lanes], value, UNSEEN)
                o_ref[:, 4 * q + 2 * part + h] = value.astype(BF16)


def z_part(kspace, mask, table):
    return pl.pallas_call(
        z_kernel,
        in_specs=[VMEM, VMEM, VMEM],
        out_specs=VMEM,
        out_shape=pltpu.VMEM((16, 17, 8, 128), BF16),
        name="z_part",
        compiler_params=SMALL,
    )(near(kspace), near(mask), near(table))


def iota(shape, dim):
    return lax.broadcasted_iota(jnp.int32, shape, dim)


def one_hot(test):
    return jnp.where(test, 1.0, 0.0).astype(BF16)


def factor_rows(r_ref):
    t = lax.axis_index("tm")
    upper = iota((8, 128), 0) < 4
    first = iota((8, 128), 1) < 32
    tiles = []
    for f in range(16):
        ahead = lax.rem(f - t + 16, 8)
        flip = lax.rem(f // 8 + t // 8, 2)
        raw = r_ref[ahead * 2 + flip, 16].astype(F32)
        re = jnp.broadcast_to(raw[0:1], (8, 128))
        im = jnp.broadcast_to(raw[1:2], (8, 128))
        tiles.append(jnp.where(first, jnp.where(upper, re, im), pltpu.roll(jnp.where(upper, -im, re), 32, 1)))
    return jnp.concatenate(tiles, axis=0).astype(BF16)


def image_kernel(r_ref, l_ref, o_ref):
    column = iota((128, 256), 1)
    pick = iota((128, 256), 0) == column // 8 + column // 4 % 2 * 32
    weights = dot(factor_rows(r_ref), one_hot(pick))
    same_x = iota((128, 256), 0) % 4 == column % 4
    weights = jnp.where(same_x, weights, 0.0).astype(BF16)
    o_ref[...] = dot(weights, l_ref[...]).reshape(16, 8, 256)


def image_part(received, spatial):
    return pl.pallas_call(
        image_kernel,
        in_specs=[VMEM, VMEM],
        out_specs=VMEM,
        out_shape=pltpu.VMEM((16, 8, 256), F32),
        name="image_part",
        compiler_params=SMALL,
    )(near(received), near(spatial))


def prepare_kernel(r_ref, w_ref, z_ref):
    row = iota((256, 128), 0)
    pick = iota((256, 128), 1) == row // 8 + row // 4 % 2 * 32
    weights = lax.dot_general(
        one_hot(pick), factor_rows(r_ref), (((1,), (1,)), ((), ())), preferred_element_type=F32
    )
    same_x = row % 4 == iota((256, 128), 1) % 4
    w_ref[...] = jnp.where(same_x, weights, 0.0).astype(BF16)

    low_half = iota((8, 128), 1) < N

    def value(v, tile):
        code = r_ref[v, tile].astype(F32)
        return jnp.where(jnp.abs(code) < SEEN_BELOW, decode(code, Z_SCALE), UNSEEN)

    def pair(v, carry):
        for q in range(4):
            for part in range(2):
                for h in range(2):
                    a, b = value(v, 4 * q + 2 * part + h), value(v + 8, 4 * q + 2 * part + h)
                    z_ref[q, part, 4 * v + 2 * h] = jnp.where(low_half, a, pltpu.roll(b, N, 1))
                    z_ref[q, part, 4 * v + 2 * h + 1] = jnp.where(low_half, pltpu.roll(a, N, 1), b)
        return carry

    lax.fori_loop(0, 8, pair, 0)


def prepare_part(received):
    return pl.pallas_call(
        prepare_kernel,
        in_specs=[VMEM],
        out_specs=[VMEM, VMEM],
        out_shape=[
            pltpu.VMEM((256, 128), BF16),
            pltpu.VMEM((4, 2, 32, 8, 128), F32),
        ],
        name="prepare_part",
        compiler_params=SMALL,
    )(near(received))


def plus(a, b):
    return a[0] + b[0], a[1] + b[1]


def minus(a, b):
    return a[0] - b[0], a[1] - b[1]


def plus_i(a, b, sign):
    if sign > 0:
        return a[0] - b[1], a[1] + b[0]
    return a[0] + b[1], a[1] - b[0]


def times(a, c, s, sign):
    if sign > 0:
        return a[0] * c - a[1] * s, a[1] * c + a[0] * s
    return a[0] * c + a[1] * s, a[1] * c - a[0] * s


def dft4(x, sign):
    a, b, c, d = plus(x[0], x[2]), minus(x[0], x[2]), plus(x[1], x[3]), minus(x[1], x[3])
    return [plus(a, c), plus_i(b, d, sign), minus(a, c), plus_i(b, d, -sign)]


def dft8(x, sign):
    half = math.sqrt(0.5)
    e, o = dft4(x[0::2], sign), dft4(x[1::2], sign)
    p = plus_i(o[1], o[1], sign)
    m = plus_i(o[3], o[3], -sign)
    p = p[0] * half, p[1] * half
    m = m[0] * half, m[1] * half
    return [
        plus(e[0], o[0]),
        plus(e[1], p),
        plus_i(e[2], o[2], sign),
        minus(e[3], m),
        minus(e[0], o[0]),
        minus(e[1], p),
        plus_i(e[2], o[2], -sign),
        plus(e[3], m),
    ]


def main_kernel(s_ref, i_ref, z_ref, f_ref, b_ref, y_ref, o_ref, t_ref, u_ref, acc_ref):
    upper = iota((8, 256), 0) < 4
    low_half = iota((8, 128), 1) < N
    flip = jnp.where(low_half, 1.0, -1.0)
    cos1 = jnp.where(low_half, 1.0, math.sqrt(0.5))
    cos3 = jnp.where(low_half, 1.0, -math.sqrt(0.5))
    sin1 = jnp.where(low_half, 0.0, math.sqrt(0.5))

    def sens(q, part, yh, h):
        at = yh * 256 + h * 128
        return s_ref[part, q, :, at : at + 128].astype(F32)

    def along_z(value, table):
        high, low = halves(value)
        table = jnp.concatenate([table[:256], table[:256], table[256:]], axis=0)
        return dot(jnp.concatenate([high, low, high], axis=1), table)

    def coil_images(q):
        parts = ([], [])
        for h in range(2):
            for yh in range(16):
                both = i_ref[yh, :, h * 128 : h * 128 + 128]
                other = pltpu.roll(both, 4, 0)
                a = jnp.where(upper[:, :128], both, other)
                b = jnp.where(upper[:, :128], other, both)
                s_re, s_im = sens(q, 0, yh, h), sens(q, 1, yh, h)
                parts[0].append(s_re * a - s_im * b)
                parts[1].append(s_re * b + s_im * a)
        value = jnp.concatenate([jnp.concatenate(part, axis=0) for part in parts], axis=1)
        t_ref[q] = along_z(value, f_ref)

    def rows(m, n):
        at = n % 2 * 128 + (2 * m + n // 2) * 8
        return slice(at, at + 8)

    def turn(value, i, sign):
        if i == 0:
            return value
        if i == 2:
            re, im = value
            if sign > 0:
                return jnp.where(low_half, re, -im), jnp.where(low_half, im, re)
            return jnp.where(low_half, re, im), jnp.where(low_half, im, -re)
        return times(value, cos1 if i == 1 else cos3, sin1, sign)

    def wave(n, j):
        at = 2 * (8 * n + j)
        return y_ref[at : at + 1, :], y_ref[at + 1 : at + 2, :]

    def across(value):
        return tuple(part * flip + pltpu.roll(part, N, 1) for part in value)

    def residual(q):
        for n in range(4):
            x = [(t_ref[q, rows(m, n), :128], t_ref[q, rows(m, n), 128:]) for m in range(8)]
            x = dft8(x, -1)
            for j in range(8):
                if j > 0:
                    x[j] = times(x[j], *wave(n, j), -1)
                u_ref[q, 4 * j + n, 0], u_ref[q, 4 * j + n, 1] = x[j]
        for j in range(8):
            x = dft4([(u_ref[q, 4 * j + n, 0], u_ref[q, 4 * j + n, 1]) for n in range(4)], -1)
            for i in range(4):
                re, im = across(turn(x[i], i, -1))
                z_re, z_im = z_ref[q, 0, 8 * i + j], z_ref[q, 1, 8 * i + j]
                seen = z_re < SEEN_BELOW
                left = jnp.where(seen, re - z_re, 0.0), jnp.where(seen, im - z_im, 0.0)
                x[i] = turn(across(left), i, 1)
            x = dft4(x, 1)
            for n in range(4):
                if j > 0:
                    x[n] = times(x[n], *wave(n, j), 1)
                u_ref[q, 4 * j + n, 0], u_ref[q, 4 * j + n, 1] = x[n]
        for n in range(4):
            x = [(u_ref[q, 4 * j + n, 0], u_ref[q, 4 * j + n, 1]) for j in range(8)]
            x = dft8(x, 1)
            for m in range(8):
                t_ref[q, rows(m, n), :128], t_ref[q, rows(m, n), 128:] = x[m]

    def combine(q):
        value = along_z(t_ref[q], b_ref)
        for h in range(2):
            for yh in range(16):
                at = h * 128 + yh * 8
                a, b = value[at : at + 8, :128], value[at : at + 8, 128:]
                s_re, s_im = sens(q, 0, yh, h), sens(q, 1, yh, h)
                re = s_re * a + s_im * b
                im = s_re * b - s_im * a
                if q > 0:
                    re = re + acc_ref[yh, h, 0]
                    im = im + acc_ref[yh, h, 1]
                if q < 3:
                    acc_ref[yh, h, 0] = re
                    acc_ref[yh, h, 1] = im
                else:
                    re = re + pltpu.roll(re, 4, 0)
                    im = im + pltpu.roll(im, 4, 0)
                    o_ref[yh, :, h * 128 : h * 128 + 128] = jnp.where(upper[:, :128], re, im)

    coil_images(0)
    for q in range(4):
        if q < 3:
            coil_images(q + 1)
        residual(q)
        if q > 0:
            combine(q - 1)
    combine(3)


def main_part(sens, images, z):
    fwd, inv = z_tables()
    return pl.pallas_call(
        main_kernel,
        in_specs=[VMEM] * 6,
        out_specs=VMEM,
        out_shape=pltpu.VMEM((16, 8, 256), F32),
        scratch_shapes=[
            pltpu.VMEM((4, 256, 256), F32),
            pltpu.VMEM((4, 32, 2, 8, 128), F32),
            pltpu.VMEM((16, 2, 2, 8, 128), F32),
        ],
        name="main_part",
        compiler_params=SMALL,
    )(
        near(sens),
        near(images),
        near(z),
        near(jnp.asarray(fwd)),
        near(jnp.asarray(inv)),
        near(jnp.asarray(y_table())),
    )


def last_kernel(w_ref, c_ref, o_ref):
    high, low = halves(c_ref[...].reshape(128, 256))
    w = w_ref[...]
    out = dot(w, high) + dot(w, low)
    for r in range(32):
        for part in range(2):
            row = r * 8 + part * 4
            o_ref[r, part] = out[row : row + 4]


def last_part(weights, combined):
    return pl.pallas_call(
        last_kernel,
        in_specs=[VMEM, VMEM],
        out_specs=VMEM,
        out_shape=jax.ShapeDtypeStruct((32, 2, 4, 256), F32),
        name="last_part",
        compiler_params=SMALL,
    )(near(weights), near(combined))


def near(value):
    return pltpu.with_memory_space_constraint(value, pltpu.VMEM)


def far(value):
    return pltpu.with_memory_space_constraint(value, pltpu.HBM)


def exchange(value, axis):
    return lax.all_to_all(value, axis, split_axis=0, concat_axis=0, tiled=True)


def sources():
    pairs = []
    for j in range(16):
        for t in range(16):
            half, place = t // 8 ^ j % 2, (t + j // 2) % 8
            source = j ^ 2 if j % 2 else j
            pairs.append((source * 16 + half * 8 + place, j * 16 + t))
    return pairs


def per_device(spatial, temporal, coil_sens, kspace, sample_mask):
    factors = lax.ppermute(temporal.transpose(1, 0, 2), ("vox", "tm"), sources())
    spatial, kspace, mask, table = load_part(spatial, kspace, sample_mask)
    z = z_part(kspace, mask, table)
    z = z.at[:, 16].set(jnp.pad(factors[0], ((0, 6), (0, 96))))
    received = exchange(z, "vox")
    images = image_part(received, spatial)
    images = exchange(images, "tm")
    weights, z = prepare_part(received)
    combined = main_part(coil_sens.reshape(2, 4, 8, 4096), images, z)
    combined = exchange(combined, "tm")
    return last_part(weights, combined)


def solution(mesh):
    placed = (
        P(None, None, "vox", "tm"),
        P(None, "tm", None),
        P(None, None, "vox", None),
        P(None, "tm", None, None, "vox"),
        P("tm", "vox"),
    )
    return jax.shard_map(
        per_device,
        mesh=mesh,
        in_specs=placed,
        out_specs=P(None, None, "vox", "tm"),
        check_vma=False,
    )
```

```python
import math

import jax
import jax.numpy as jnp
import numpy as np
from jax import lax
from jax.experimental import pallas as pl
from jax.experimental.pallas import tpu as pltpu
from jax.sharding import PartitionSpec as P


N = 64
F32 = jnp.float32
BF16 = jnp.bfloat16
VMEM = pl.BlockSpec(memory_space=pltpu.VMEM)
HBM = pl.BlockSpec(memory_space=pl.ANY)
SMALL = pltpu.CompilerParams(vmem_limit_bytes=16 * 2**20)
Z_SCALE = 2.0**6
IMAGE_SCALE = 2.0**4
UNSEEN = 3e38
SEEN_BELOW = 1e37


def split(table):
    table = np.asarray(table, np.float64)
    high = table.astype(jnp.bfloat16)
    low = (table - high.astype(np.float64)).astype(jnp.bfloat16)
    return high, low


def dft64():
    k = np.arange(N)
    angle = 2.0 * np.pi * (np.outer(k, k) % N) / N
    return np.cos(angle), np.sin(angle)


def x_table():
    cos, sin = dft64()
    table = np.zeros((2, 16, 2, 4, 2, 2, N))
    for c in range(2):
        table[0, :, c, :, c, 0] = cos.reshape(16, 4, N)
        table[0, :, c, :, c, 1] = -sin.reshape(16, 4, N)
        table[1, :, c, :, c, 0] = sin.reshape(16, 4, N)
        table[1, :, c, :, c, 1] = cos.reshape(16, 4, N)
    return np.concatenate(split(table.reshape(256, 256) / 8.0 * Z_SCALE), axis=1)


def z_tables():
    cos, sin = dft64()
    tables = []
    for sign in (1.0, -1.0):
        table = np.zeros((2, 2, N, 2, 2, N))
        for b in range(2):
            table[0, b, :, 0, b] = cos
            table[1, b, :, 0, b] = sign * sin
            table[0, b, :, 1, b] = -sign * sin
            table[1, b, :, 1, b] = cos
        high, low = split(table.reshape(256, 256) / 64.0)
        tables.append(np.concatenate([high, low], axis=0))
    return tables


def y_table():
    n, j, b = np.meshgrid(np.arange(4), np.arange(8), np.arange(128) // N, indexing="ij")
    angle = 2.0 * np.pi * ((2 * n + b) * j % N) / N
    return np.stack([np.cos(angle), np.sin(angle)], axis=2).reshape(64, 128).astype(np.float32)


def dot(a, b):
    return jnp.dot(a, b, preferred_element_type=F32)


def halves(value):
    high = value.astype(BF16)
    return high, (value - high.astype(F32)).astype(BF16)


def load_kernel(l_hbm, k_hbm, m_hbm, t_hbm, l_ref, k_ref, m_ref, t_ref, s_ref, sems):
    copies = [
        pltpu.make_async_copy(l_hbm, s_ref, sems.at[0]),
        pltpu.make_async_copy(m_hbm, m_ref, sems.at[1]),
        pltpu.make_async_copy(t_hbm, t_ref, sems.at[2]),
        pltpu.make_async_copy(k_hbm, k_ref, sems.at[3]),
    ]
    for copy in copies:
        copy.start()
    copies[0].wait()
    for r in range(0, 32, 2):
        rows = [s_ref[r + i // 2, i % 2].astype(F32) for i in range(4)]
        l_ref[8 * r : 8 * r + 16] = jnp.concatenate(rows, axis=0).astype(BF16)
    for copy in copies[1:]:
        copy.wait()


def load_part(spatial, kspace, mask):
    return pl.pallas_call(
        load_kernel,
        in_specs=[HBM] * 4,
        out_specs=[VMEM] * 4,
        out_shape=[
            pltpu.VMEM((256, 256), BF16),
            pltpu.VMEM(kspace.shape, BF16),
            pltpu.VMEM((1, 256), jnp.int32),
            pltpu.VMEM((256, 512), BF16),
        ],
        scratch_shapes=[
            pltpu.VMEM(spatial.shape, BF16),
            pltpu.SemaphoreType.DMA((4,)),
        ],
        name="load_part",
        compiler_params=SMALL,
    )(far(spatial), far(kspace), far(mask), far(jnp.asarray(x_table())))


def encode(value):
    even = value * value
    fourth = even * even
    even = fourth * fourth * even
    return jnp.where(value < 0.0, -even, even)


def decode(code, scale):
    size = jnp.abs(code)
    root = jnp.exp2(jnp.log2(size) * 0.1 - math.log2(scale))
    root = jnp.where(size > 0.0, root, 0.0)
    return jnp.where(code < 0.0, -root, root)


def z_kernel(k_ref, m_ref, t_ref, o_ref):
    seen = jnp.broadcast_to(m_ref[...].astype(F32), (8, 256)) > 0.5
    for q in range(4):
        data = [k_ref[part, 0, 2 * q + c] for c in range(2) for part in range(2)]
        out = dot(t_ref[...], jnp.concatenate(data + data, axis=0))
        out = encode(out)
        for part in range(2):
            for h in range(2):
                lanes = slice(h * 128, h * 128 + 128)
                value = out[part * 128 : part * 128 + 128, lanes].reshape(16, 8, 128)
                value = jnp.where(seen[None, :, lanes], value, UNSEEN)
                o_ref[:, 4 * q + 2 * part + h] = value.astype(BF16)


def z_part(kspace, mask, table):
    return pl.pallas_call(
        z_kernel,
        in_specs=[VMEM, VMEM, VMEM],
        out_specs=VMEM,
        out_shape=pltpu.VMEM((16, 17, 8, 128), BF16),
        name="z_part",
        compiler_params=SMALL,
    )(near(kspace), near(mask), near(table))


def iota(shape, dim):
    return lax.broadcasted_iota(jnp.int32, shape, dim)


def one_hot(test):
    return jnp.where(test, 1.0, 0.0).astype(BF16)


def factor_rows(r_ref):
    t = lax.axis_index("tm")
    upper = iota((8, 128), 0) < 4
    first = iota((8, 128), 1) < 32
    tiles = []
    for f in range(16):
        ahead = lax.rem(f - t + 16, 8)
        flip = lax.rem(f // 8 + t // 8, 2)
        raw = r_ref[ahead * 2 + flip, 16].astype(F32)
        re = jnp.broadcast_to(raw[0:1], (8, 128))
        im = jnp.broadcast_to(raw[1:2], (8, 128))
        tiles.append(jnp.where(first, jnp.where(upper, re, im), pltpu.roll(jnp.where(upper, -im, re), 32, 1)))
    return jnp.concatenate(tiles, axis=0).astype(BF16)


def image_kernel(r_ref, l_ref, o_ref):
    column = iota((128, 256), 1)
    pick = iota((128, 256), 0) == column // 8 + column // 4 % 2 * 32
    weights = dot(factor_rows(r_ref), one_hot(pick))
    same_x = iota((128, 256), 0) % 4 == column % 4
    weights = jnp.where(same_x, weights, 0.0).astype(BF16)
    o_ref[...] = encode(dot(weights, l_ref[...]) * IMAGE_SCALE).reshape(16, 8, 256).astype(BF16)


def image_part(received, spatial):
    return pl.pallas_call(
        image_kernel,
        in_specs=[VMEM, VMEM],
        out_specs=VMEM,
        out_shape=pltpu.VMEM((16, 8, 256), BF16),
        name="image_part",
        compiler_params=SMALL,
    )(near(received), near(spatial))


def prepare_kernel(r_ref, w_ref, z_ref):
    row = iota((256, 128), 0)
    pick = iota((256, 128), 1) == row // 8 + row // 4 % 2 * 32
    weights = lax.dot_general(
        one_hot(pick), factor_rows(r_ref), (((1,), (1,)), ((), ())), preferred_element_type=F32
    )
    same_x = row % 4 == iota((256, 128), 1) % 4
    w_ref[...] = jnp.where(same_x, weights, 0.0).astype(BF16)

    low_half = iota((8, 128), 1) < N

    def value(v, tile):
        code = r_ref[v, tile].astype(F32)
        return jnp.where(jnp.abs(code) < SEEN_BELOW, decode(code, Z_SCALE), UNSEEN)

    def pair(v, carry):
        for q in range(4):
            for part in range(2):
                for h in range(2):
                    a, b = value(v, 4 * q + 2 * part + h), value(v + 8, 4 * q + 2 * part + h)
                    z_ref[q, part, 4 * v + 2 * h] = jnp.where(low_half, a, pltpu.roll(b, N, 1))
                    z_ref[q, part, 4 * v + 2 * h + 1] = jnp.where(low_half, pltpu.roll(a, N, 1), b)
        return carry

    lax.fori_loop(0, 8, pair, 0)


def prepare_part(received):
    return pl.pallas_call(
        prepare_kernel,
        in_specs=[VMEM],
        out_specs=[VMEM, VMEM],
        out_shape=[
            pltpu.VMEM((256, 128), BF16),
            pltpu.VMEM((4, 2, 32, 8, 128), F32),
        ],
        name="prepare_part",
        compiler_params=SMALL,
    )(near(received))


def plus(a, b):
    return a[0] + b[0], a[1] + b[1]


def minus(a, b):
    return a[0] - b[0], a[1] - b[1]


def plus_i(a, b, sign):
    if sign > 0:
        return a[0] - b[1], a[1] + b[0]
    return a[0] + b[1], a[1] - b[0]


def times(a, c, s, sign):
    if sign > 0:
        return a[0] * c - a[1] * s, a[1] * c + a[0] * s
    return a[0] * c + a[1] * s, a[1] * c - a[0] * s


def dft4(x, sign):
    a, b, c, d = plus(x[0], x[2]), minus(x[0], x[2]), plus(x[1], x[3]), minus(x[1], x[3])
    return [plus(a, c), plus_i(b, d, sign), minus(a, c), plus_i(b, d, -sign)]


def dft8(x, sign):
    half = math.sqrt(0.5)
    e, o = dft4(x[0::2], sign), dft4(x[1::2], sign)
    p = plus_i(o[1], o[1], sign)
    m = plus_i(o[3], o[3], -sign)
    p = p[0] * half, p[1] * half
    m = m[0] * half, m[1] * half
    return [
        plus(e[0], o[0]),
        plus(e[1], p),
        plus_i(e[2], o[2], sign),
        minus(e[3], m),
        minus(e[0], o[0]),
        minus(e[1], p),
        plus_i(e[2], o[2], -sign),
        plus(e[3], m),
    ]


def main_kernel(s_ref, i_ref, z_ref, f_ref, b_ref, y_ref, o_ref, x_ref, t_ref, u_ref, acc_ref):
    upper = iota((8, 256), 0) < 4
    low_half = iota((8, 128), 1) < N
    flip = jnp.where(low_half, 1.0, -1.0)
    cos1 = jnp.where(low_half, 1.0, math.sqrt(0.5))
    cos3 = jnp.where(low_half, 1.0, -math.sqrt(0.5))
    sin1 = jnp.where(low_half, 0.0, math.sqrt(0.5))

    def sens(q, part, yh, h):
        at = yh * 256 + h * 128
        return s_ref[part, q, :, at : at + 128].astype(F32)

    def along_z(value, table):
        high, low = halves(value)
        table = jnp.concatenate([table[:256], table[:256], table[256:]], axis=0)
        return dot(jnp.concatenate([high, low, high], axis=1), table)

    def coil_images(q):
        parts = ([], [])
        for h in range(2):
            for yh in range(16):
                both = x_ref[yh, :, h * 128 : h * 128 + 128]
                other = pltpu.roll(both, 4, 0)
                a = jnp.where(upper[:, :128], both, other)
                b = jnp.where(upper[:, :128], other, both)
                s_re, s_im = sens(q, 0, yh, h), sens(q, 1, yh, h)
                parts[0].append(s_re * a - s_im * b)
                parts[1].append(s_re * b + s_im * a)
        value = jnp.concatenate([jnp.concatenate(part, axis=0) for part in parts], axis=1)
        t_ref[q] = along_z(value, f_ref)

    def rows(m, n):
        at = n % 2 * 128 + (2 * m + n // 2) * 8
        return slice(at, at + 8)

    def turn(value, i, sign):
        if i == 0:
            return value
        if i == 2:
            re, im = value
            if sign > 0:
                return jnp.where(low_half, re, -im), jnp.where(low_half, im, re)
            return jnp.where(low_half, re, im), jnp.where(low_half, im, -re)
        return times(value, cos1 if i == 1 else cos3, sin1, sign)

    def wave(n, j):
        at = 2 * (8 * n + j)
        return y_ref[at : at + 1, :], y_ref[at + 1 : at + 2, :]

    def across(value):
        return tuple(part * flip + pltpu.roll(part, N, 1) for part in value)

    def residual(q):
        for n in range(4):
            x = [(t_ref[q, rows(m, n), :128], t_ref[q, rows(m, n), 128:]) for m in range(8)]
            x = dft8(x, -1)
            for j in range(8):
                if j > 0:
                    x[j] = times(x[j], *wave(n, j), -1)
                u_ref[q, 4 * j + n, 0], u_ref[q, 4 * j + n, 1] = x[j]
        for j in range(8):
            x = dft4([(u_ref[q, 4 * j + n, 0], u_ref[q, 4 * j + n, 1]) for n in range(4)], -1)
            for i in range(4):
                re, im = across(turn(x[i], i, -1))
                z_re, z_im = z_ref[q, 0, 8 * i + j], z_ref[q, 1, 8 * i + j]
                seen = z_re < SEEN_BELOW
                left = jnp.where(seen, re - z_re, 0.0), jnp.where(seen, im - z_im, 0.0)
                x[i] = turn(across(left), i, 1)
            x = dft4(x, 1)
            for n in range(4):
                if j > 0:
                    x[n] = times(x[n], *wave(n, j), 1)
                u_ref[q, 4 * j + n, 0], u_ref[q, 4 * j + n, 1] = x[n]
        for n in range(4):
            x = [(u_ref[q, 4 * j + n, 0], u_ref[q, 4 * j + n, 1]) for j in range(8)]
            x = dft8(x, 1)
            for m in range(8):
                t_ref[q, rows(m, n), :128], t_ref[q, rows(m, n), 128:] = x[m]

    def combine(q):
        value = along_z(t_ref[q], b_ref)
        for h in range(2):
            for yh in range(16):
                at = h * 128 + yh * 8
                a, b = value[at : at + 8, :128], value[at : at + 8, 128:]
                s_re, s_im = sens(q, 0, yh, h), sens(q, 1, yh, h)
                re = s_re * a + s_im * b
                im = s_re * b - s_im * a
                if q > 0:
                    re = re + acc_ref[yh, h, 0]
                    im = im + acc_ref[yh, h, 1]
                if q < 3:
                    acc_ref[yh, h, 0] = re
                    acc_ref[yh, h, 1] = im
                else:
                    re = re + pltpu.roll(re, 4, 0)
                    im = im + pltpu.roll(im, 4, 0)
                    o_ref[yh, :, h * 128 : h * 128 + 128] = jnp.where(upper[:, :128], re, im)

    for yh in range(16):
        x_ref[yh] = decode(i_ref[yh].astype(F32), IMAGE_SCALE)
    coil_images(0)
    for q in range(4):
        if q < 3:
            coil_images(q + 1)
        residual(q)
        if q > 0:
            combine(q - 1)
    combine(3)


def main_part(sens, images, z):
    fwd, inv = z_tables()
    return pl.pallas_call(
        main_kernel,
        in_specs=[VMEM] * 6,
        out_specs=VMEM,
        out_shape=pltpu.VMEM((16, 8, 256), F32),
        scratch_shapes=[
            pltpu.VMEM((16, 8, 256), F32),
            pltpu.VMEM((4, 256, 256), F32),
            pltpu.VMEM((4, 32, 2, 8, 128), F32),
            pltpu.VMEM((16, 2, 2, 8, 128), F32),
        ],
        name="main_part",
        compiler_params=SMALL,
    )(
        near(sens),
        near(images),
        near(z),
        near(jnp.asarray(fwd)),
        near(jnp.asarray(inv)),
        near(jnp.asarray(y_table())),
    )


def last_kernel(w_ref, c_ref, o_ref):
    high, low = halves(c_ref[...].reshape(128, 256))
    w = w_ref[...]
    out = dot(w, high) + dot(w, low)
    for r in range(32):
        for part in range(2):
            row = r * 8 + part * 4
            o_ref[r, part] = out[row : row + 4]


def last_part(weights, combined):
    return pl.pallas_call(
        last_kernel,
        in_specs=[VMEM, VMEM],
        out_specs=VMEM,
        out_shape=jax.ShapeDtypeStruct((32, 2, 4, 256), F32),
        name="last_part",
        compiler_params=SMALL,
    )(near(weights), near(combined))


def near(value):
    return pltpu.with_memory_space_constraint(value, pltpu.VMEM)


def far(value):
    return pltpu.with_memory_space_constraint(value, pltpu.HBM)


def exchange(value, axis):
    return lax.all_to_all(value, axis, split_axis=0, concat_axis=0, tiled=True)


def sources():
    pairs = []
    for j in range(16):
        for t in range(16):
            half, place = t // 8 ^ j % 2, (t + j // 2) % 8
            source = j ^ 2 if j % 2 else j
            pairs.append((source * 16 + half * 8 + place, j * 16 + t))
    return pairs


def per_device(spatial, temporal, coil_sens, kspace, sample_mask):
    factors = lax.ppermute(temporal.transpose(1, 0, 2), ("vox", "tm"), sources())
    spatial, kspace, mask, table = load_part(spatial, kspace, sample_mask)
    z = z_part(kspace, mask, table)
    z = z.at[:, 16].set(jnp.pad(factors[0], ((0, 6), (0, 96))))
    received = exchange(z, "vox")
    images = image_part(received, spatial)
    images = exchange(images, "tm")
    weights, z = prepare_part(received)
    combined = main_part(coil_sens.reshape(2, 4, 8, 4096), images, z)
    combined = exchange(combined, "tm")
    return last_part(weights, combined)


def solution(mesh):
    placed = (
        P(None, None, "vox", "tm"),
        P(None, "tm", None),
        P(None, None, "vox", None),
        P(None, "tm", None, None, "vox"),
        P("tm", "vox"),
    )
    return jax.shard_map(
        per_device,
        mesh=mesh,
        in_specs=placed,
        out_specs=P(None, None, "vox", "tm"),
        check_vma=False,
    )
```
